128 devices in a mesh: seq: 32 (over z, x, core), mp: 4 (over y).
Axes of the slice: x: 4, y: 4, z: 4, core: 2. Of those that a mesh axis runs over, the one named last changes fastest.
Arguments:
- queries: bfloat16 [32768, 4096], P('seq', 'mp'), may hold values from -20 to 20
- image_keys: bfloat16 [32, 768, 512], P('seq', None, 'mp'), may hold values from -5 to 5
- image_values: bfloat16 [32, 768, 512], P('seq', None, 'mp'), may hold values from -80 to 80
- span_tiles: int32 [1024, 1], P('seq'), may hold values from 0 to 31; in each aligned block of 32 rows (0 to 31, 32 to 63, ...) at most 2 rows name the same one
- gate_logit: float32 [1], replicated, may hold values from 0.3 to 1.5
- cotangent: bfloat16 [32768, 4096], P('seq', 'mp'), may hold values from -36 to 36
Outputs:
- attended: bfloat16 [32768, 4096], P('seq', 'mp')
- query_grad: bfloat16 [32768, 4096], P('seq', 'mp')
- key_grad: bfloat16 [32, 768, 512], P('seq', None, 'mp')
- value_grad: bfloat16 [32, 768, 512], P('seq', None, 'mp')
- gate_grad: float32 [1], replicated
The draws below stay inside these ranges and needn't reach their ends.
Inputs may be any that keep to these rules, and one draw needn't show every extreme that they name: `span_tiles`: among the 32 spans of one index of seq, at most 2 reference the same tile, and that bound is reached; every tile is referenced by some span.
All inputs are finite; a program needn't handle non-finite values.
Results may differ from the reference program's by a relative error of at most 0.012.
The reference program's roundings to bfloat16 on the way (of `probs_b`, `attn`, `attn_grad` and `dscore`) count: a program that leaves them out, or rounds other values in their place, can miss the bound.
Values may be sent and summed in bfloat16 or wider, within the bound.
A program may use at most 192 MiB of HBM per device.

```python
import math
import jax
import jax.numpy as jnp
import numpy as np
from jax import lax

HEADS = 32
KV_HEADS = 4
HEAD = 128
IMG = 768
SPAN = 32
SPANS_DEV = 32
TOKENS = 32768
SPANS = 1024
TILES = 32
CAP = 2
SLOTS = 64
KVD = 512


def draw_queries(key, part):
    columns = HEADS * HEAD
    drawn_rows = jnp.clip(jax.random.normal(jax.random.fold_in(key, 1), (TOKENS, columns), jnp.float32), -5.0, 5.0)
    return drawn_rows.astype(jnp.bfloat16)


def draw_image_keys(key, part):
    kv_columns = KV_HEADS * HEAD
    drawn_rows = jnp.clip(jax.random.normal(jax.random.fold_in(key, 4), (TILES, IMG, kv_columns), jnp.float32), -5.0, 5.0)
    return drawn_rows.astype(jnp.bfloat16)


def draw_cotangent(key, part):
    columns = HEADS * HEAD
    drawn_rows = jnp.clip(jax.random.normal(jax.random.fold_in(key, 6), (TOKENS, columns), jnp.float32), -4.0, 4.0)
    row_rise = 1.0 + 2.0 * jnp.arange(TOKENS, dtype=jnp.float32) / TOKENS
    column_rise = 1.0 + 2.0 * jnp.arange(columns, dtype=jnp.float32) / columns
    return (drawn_rows * row_rise[:, None] * column_rise[None, :]).astype(jnp.bfloat16)


def level_of(key, extent, cuts, low, largest):
    def one(position, shards_of):
        draws = jax.random.uniform(jax.random.fold_in(jax.random.fold_in(key, 6), position), (shards_of,), jnp.float32, low / len(cuts), largest / len(cuts))
        return jnp.repeat(jnp.exp(draws), extent[position] // shards_of).reshape((-1,) + (1,) * (len(extent) - position - 1))

    level = one(*cuts[0])
    for cut in cuts[1:]:
        level = level * one(*cut)
    return level


def deal_out(stream_key, own, number, rows, amount, top, most, slope):
    order = jax.random.permutation(stream_key, amount)
    heavy_load, ordinary = portions_of(amount, rows * top, most, slope, True), portions_of(amount, rows * top, most, slope, False)
    places = jnp.arange(amount)

    def named(tallies, offset_by):
        used = int((tallies > 0).sum())
        fixed = max(1, used // 4)
        shifted = fixed + (places - fixed + offset_by * (used - fixed)) % max(1, amount - fixed)
        return jnp.zeros((amount,), jnp.int32).at[order[jnp.where(places < fixed, places, shifted)]].set(jnp.asarray(tallies, jnp.int32))

    tallies = jnp.where(number % 4 == 0, named(heavy_load, number // 4), named(ordinary, number - number // 4 - 1))
    mixed = jax.random.permutation(jax.random.fold_in(own, 3), amount)
    giver, receiver = mixed[0:amount // 2 * 2:2], mixed[1:amount // 2 * 2:2]
    slack = jnp.minimum(tallies[giver] - 1, most - tallies[receiver]) // 2
    slack = jnp.where((giver == order[0]) | (receiver == order[0]) | (tallies[receiver] == 0), 0, jnp.maximum(slack, 0))
    shifted = jax.random.randint(jax.random.fold_in(own, 4), (amount // 2,), 0, 1 << 20) % (slack + 1)
    tallies = tallies.at[giver].add(-shifted).at[receiver].add(shifted)
    labels = jnp.searchsorted(jnp.cumsum(tallies), jnp.arange(rows * top), side="right").astype(jnp.int32)
    listing = labels.reshape(top, rows).T
    listing = listing[jax.random.permutation(jax.random.fold_in(own, 1), rows)]
    offset_by = jax.random.randint(jax.random.fold_in(own, 2), (rows, 1), 0, top)
    return jnp.take_along_axis(listing, (jnp.arange(top)[None, :] + offset_by) % top, axis=1)


def portions_of(amount, total, limit, lean, full):
    weights = [(1 << 20) // math.isqrt(rank ** lean) + 1 for rank in range(1, amount + 1)]
    largest = limit if full else min(limit, max(-(-total // amount), total * weights[0] // sum(weights)))
    least = 1 if total - largest >= amount - 1 else 0
    holding, surplus = [largest] + [least] * (amount - 1), total - largest - least * (amount - 1)
    while surplus > 0:
        free = [i for i in range(1, amount) if holding[i] < largest] or [i for i in range(1, amount) if holding[i] < limit]
        pool, left = sum([weights[i] for i in free]), surplus
        for i in free:
            extra = min(limit - holding[i], max(1, left * weights[i] // pool), surplus)
            holding[i] = holding[i] + extra
            surplus = surplus - extra
    return np.array(holding)


def scatter_about(key, dims, deviation, reach, cuts=(), held_as=jnp.bfloat16):
    result = jax.random.normal(key, dims, jnp.float32) * deviation
    if len(cuts) > 0:
        result = level_of(key, dims, cuts, -0.22, 0.18) * result
    return jnp.clip(result, min=-reach, max=reach).astype(held_as)


def setup_inputs(seed: int = 0) -> dict:
    key_of = jax.random.split(jax.random.key(seed), 7)
    queries = draw_queries(jax.random.fold_in(key_of[6], 71), 0)
    image_keys = draw_image_keys(jax.random.fold_in(key_of[6], 71), 0)
    image_values = scatter_about(key_of[2], (TILES, IMG, KVD), 16.0, 80.0, ((0, 32), (2, 4)))
    span_tiles_keys = jax.random.split(jax.random.fold_in(key_of[3], 1), SPANS // SPANS_DEV)
    span_tiles_turns = jax.random.permutation(jax.random.fold_in(key_of[3], 3), SPANS // SPANS_DEV)
    span_tiles = jax.vmap(lambda own, number: deal_out(jax.random.fold_in(key_of[3], 2), own, number, SPANS_DEV, TILES, 1, CAP, 2))(span_tiles_keys, span_tiles_turns).reshape((SPANS, 1))
    gate_logit = jnp.clip(jax.random.uniform(key_of[4], (1,), jnp.float32, 0.3, 1.5), 0.3, 1.5)
    cotangent = draw_cotangent(jax.random.fold_in(key_of[6], 71), 0)
    return {"queries": queries, "image_keys": image_keys, "image_values": image_values, "span_tiles": span_tiles, "gate_logit": gate_logit, "cotangent": cotangent}


def reference(queries, image_keys, image_values, span_tiles, gate_logit, cotangent):
    score_scale = 1.0 / math.sqrt(HEAD)
    columns = HEADS * HEAD
    kv_columns = KV_HEADS * HEAD
    group = HEADS // KV_HEADS
    gate_tanh = jnp.tanh(gate_logit[0])
    owners = span_tiles[:, 0]
    query_spans = queries.reshape(SPANS, SPAN, columns)
    attn_grad = (gate_tanh * cotangent.astype(jnp.float32)).astype(jnp.bfloat16)
    grad_spans = attn_grad.reshape(SPANS, SPAN, columns)
    nought = jnp.zeros((), jnp.bfloat16)

    def per_tile(accums, tile_index):
        attended_all, qgrad_all = accums
        order_keys = jnp.where(owners == tile_index, 0, 1).astype(jnp.int32)
        picked = jnp.argsort(order_keys, stable=True)[:SLOTS].astype(jnp.int32)
        is_valid = (owners[picked] == tile_index)[:, None, None]
        query_sel = jnp.where(is_valid, query_spans[picked], nought)
        grad_sel = jnp.where(is_valid, grad_spans[picked], nought)
        query_f = query_sel.reshape(SLOTS * SPAN, KV_HEADS, group, HEAD).astype(jnp.float32)
        grad_f = grad_sel.reshape(SLOTS * SPAN, KV_HEADS, group, HEAD).astype(jnp.float32)
        key_tile = image_keys[tile_index].reshape(IMG, KV_HEADS, HEAD).astype(jnp.float32)
        value_tile = image_values[tile_index].reshape(IMG, KV_HEADS, HEAD).astype(jnp.float32)
        scores = jnp.einsum('rngd,knd->ngrk', query_f, key_tile) * score_scale
        row_max = lax.optimization_barrier(jnp.max(scores, axis=3, keepdims=True))
        expo_terms = jnp.exp(scores - row_max)
        probs = expo_terms / lax.optimization_barrier(jnp.sum(expo_terms, axis=3, keepdims=True))
        probs_b = lax.optimization_barrier(probs.astype(jnp.bfloat16)).astype(jnp.float32)
        attn = jnp.einsum('ngrk,knd->rngd', probs_b, value_tile).astype(jnp.bfloat16)
        row_delta = lax.optimization_barrier(jnp.sum(grad_f * attn.astype(jnp.float32), axis=3))
        prob_grad = jnp.einsum('rngd,knd->ngrk', grad_f, value_tile)
        delta_t = jnp.transpose(row_delta, (1, 2, 0))[:, :, :, None]
        dscore = (probs * (prob_grad - delta_t) * score_scale).astype(jnp.bfloat16)
        dscore = lax.optimization_barrier(dscore).astype(jnp.float32)
        qgrad = jnp.einsum('ngrk,knd->rngd', dscore, key_tile).astype(jnp.bfloat16)
        kgrad = jnp.einsum('ngrk,rngd->knd', dscore, query_f).astype(jnp.bfloat16)
        vgrad = jnp.einsum('ngrk,rngd->knd', probs_b, grad_f).astype(jnp.bfloat16)
        attended_all = attended_all.at[picked].add(jnp.where(is_valid, attn.reshape(SLOTS, SPAN, columns), nought))
        qgrad_all = qgrad_all.at[picked].add(jnp.where(is_valid, qgrad.reshape(SLOTS, SPAN, columns), nought))
        return ((attended_all, qgrad_all), (kgrad.reshape(IMG, kv_columns), vgrad.reshape(IMG, kv_columns)))
    start = (jnp.zeros((SPANS, SPAN, columns), jnp.bfloat16), jnp.zeros((SPANS, SPAN, columns), jnp.bfloat16))
    (attended_all, qgrad_all), (key_grad, value_grad) = lax.scan(per_tile, start, jnp.arange(TILES, dtype=jnp.int32))
    attn_rows = attended_all.reshape(TOKENS, columns)
    attended = (gate_tanh * attn_rows.astype(jnp.float32)).astype(jnp.bfloat16)
    grand_total = jnp.sum(cotangent.astype(jnp.float32) * attn_rows.astype(jnp.float32))
    gate_grad = ((1.0 - gate_tanh * gate_tanh) * grand_total / math.sqrt(TOKENS * HEADS * HEAD)).reshape(1)
    return (attended, qgrad_all.reshape(TOKENS, columns), key_grad, value_grad, gate_grad)
```

```python
import functools
import math

import jax
import jax.numpy as jnp
from jax import lax
from jax.experimental import pallas as pl
from jax.experimental.pallas import tpu as pltpu
from jax.sharding import PartitionSpec as P

HEAD = 128
RING = 4
MESH = pl.DeviceIdType.MESH
F32 = jnp.float32
BF16 = jnp.bfloat16


def nt(left, right):
    return lax.dot_general(left, right, (((1,), (1,)), ((), ())), preferred_element_type=F32)


def nn(left, right):
    return lax.dot_general(left, right, (((1,), (0,)), ((), ())), preferred_element_type=F32)


def tn(left, right):
    return lax.dot_general(left, right, (((0,), (0,)), ((), ())), preferred_element_type=F32)


def wrap(value):
    return lax.rem(value + RING, RING)


def kernel(
    sizes,
    tiles,
    slots,
    gate,
    q_hbm,
    k_hbm,
    v_hbm,
    c_hbm,
    att_hbm,
    dq_hbm,
    dk_hbm,
    dv_hbm,
    gate_out,
    kall,
    vall,
    probs,
    qv,
    cv,
    qs,
    gs,
    part,
    l3,
    lb1,
    lb2,
    la1,
    la2,
    l0,
    gacc,
    gland,
    send,
    recv,
    loc,
):
    spans, span_len, heads, image_len, total_elems = sizes
    scale = 1.0 / math.sqrt(HEAD)
    me = lax.axis_index("seq")
    my = lax.axis_index("mp")
    z = lax.div(me, 8)
    x = lax.rem(lax.div(me, 2), RING)
    c = lax.rem(me, 2)
    mate = me + 1 - 2 * c
    a = z * (1 - c) + x * c
    b = x * (1 - c) + z * c
    stride_a = 4 - 3 * c
    stride_b = 1 + 3 * c

    def pair(da, db):
        return wrap(a + da) * stride_a + wrap(b + db) * stride_b

    def mate_pair(da, db):
        return wrap(b + da) * stride_b + wrap(a + db) * stride_a

    def at(da, db):
        return (2 * pair(da, db) + c, my)

    barrier = pltpu.get_barrier_semaphore()
    friends = [(mate, my)]
    for d in range(1, RING):
        friends.append((8 * wrap(z + d) + 2 * x + c, my))
        friends.append((8 * z + 2 * wrap(x + d) + c, my))
        friends.append((me, wrap(my + d)))
    for friend in friends:
        pl.semaphore_signal(barrier, inc=1, device_id=friend, device_id_type=MESH)

    k_in = pltpu.make_async_copy(k_hbm, kall.at[pl.ds(me, 1)], loc.at[0])
    v_in = pltpu.make_async_copy(v_hbm, vall.at[pl.ds(me, 1)], loc.at[1])
    q_in = pltpu.make_async_copy(q_hbm, qv, loc.at[2])
    c_in = pltpu.make_async_copy(c_hbm, cv, loc.at[3])
    k_in.start()
    q_in.start()
    c_in.start()
    v_in.start()
    pl.semaphore_wait(barrier, len(friends))

    started = []

    def remote(src, dst, index, target):
        return pltpu.make_async_remote_copy(
            src_ref=src,
            dst_ref=dst,
            send_sem=send.at[index],
            recv_sem=recv.at[index],
            device_id=target,
            device_id_type=MESH,
        )

    def start(make):
        make().start()
        started.append(make)

    half = image_len // 2
    quarter = half // 2
    steps = (0, -1, 1, 2)

    def gather(buf, base):
        mine, other = c * half, (1 - c) * half

        def piece(which, first, rows):
            return buf.at[pl.ds(2 * which, 2), pl.ds(pl.multiple_of(first, 64), rows), :]

        def own_copy(first, tile, index):
            ref = buf.at[pl.ds(tile, 1), pl.ds(pl.multiple_of(first, 64), half), :]
            return remote(ref, ref, base + index, (mate, my))

        def moved(which, direction, index, target, narrow):
            if narrow:
                ref = piece(which, mine + direction * quarter, quarter)
            else:
                ref = piece(which, mine, half)
            return remote(ref, ref, base + index, target)

        def to_mate(k, kb):
            ref = piece(pair(steps[k], steps[kb]), mine, half)
            return remote(ref, ref, base + 24 + 4 * k + kb, (mate, my))

        def from_mate(k, kb):
            ref = piece(mate_pair(steps[k], steps[kb]), other, half)
            return remote(ref, ref, base + 24 + 4 * k + kb, (mate, my))

        sign = (1, -1)

        def e0():
            start(lambda: own_copy(other, me, 0))
            start(lambda: own_copy(mine, me, 1))

        def send_b(k):
            for d in range(2):
                start(lambda d=d: moved(pair(steps[k], 0), d, 8 + 4 * k + d, at(0, sign[d]), False))

        def e1():
            own_copy(mine, mate, 0).wait_recv()
            for d in range(2):
                start(lambda d=d: moved(pair(0, 0), d, 2 + d, at(sign[d], 0), False))
            send_b(0)

        def e_a(d):
            moved(pair(-sign[d], 0), d, 2 + d, at(sign[d], 0), False).wait_recv()
            start(lambda: moved(pair(-sign[d], 0), d, 4 + d, at(sign[d], 0), True))
            send_b(1 + d)
            start(lambda: to_mate(1 + d, 0))

        def e_aq():
            for d in range(2):
                moved(pair(2, 0), d, 4 + d, at(sign[d], 0), True).wait_recv()
            send_b(3)
            start(lambda: to_mate(3, 0))

        def e_b(k, d):
            moved(pair(steps[k], -sign[d]), d, 8 + 4 * k + d, at(0, sign[d]), False).wait_recv()
            start(
                lambda: moved(
                    pair(steps[k], -sign[d]), d, 10 + 4 * k + d, at(0, sign[d]), True
                )
            )
            start(lambda: to_mate(k, 1 + d))

        def e_bq(k):
            for d in range(2):
                moved(pair(steps[k], 2), d, 10 + 4 * k + d, at(0, sign[d]), True).wait_recv()
            start(lambda: to_mate(k, 3))

        def e_end():
            own_copy(other, mate, 1).wait_recv()
            for k in range(4):
                for kb in range(4):
                    if k or kb:
                        from_mate(k, kb).wait_recv()

        events = [
            lambda: e_a(0),
            lambda: e_a(1),
            lambda: e_b(0, 0),
            lambda: e_b(0, 1),
            e_aq,
            lambda: e_bq(0),
            lambda: e_b(1, 0),
            lambda: e_b(1, 1),
            lambda: e_b(2, 0),
            lambda: e_b(2, 1),
            lambda: e_bq(1),
            lambda: e_b(3, 0),
            lambda: e_b(3, 1),
            lambda: e_bq(2),
            lambda: e_bq(3),
        ]
        return e0, e1, events, e_end

    lane_half = HEAD // 2
    lane_quarter = HEAD // 4

    def reduce(y, base):
        mine, other = c * lane_half, (1 - c) * lane_half

        def piece(which, first, rows):
            return part.at[y, pl.ds(2 * which, 2), pl.ds(pl.multiple_of(first, 32), rows), :]

        def to_mate(which):
            return remote(piece(which, other, lane_half), l3.at[y, which], base + which, (mate, my))

        def add(which, first, rows, *landed):
            view = (y, pl.ds(2 * which, 2), pl.ds(pl.multiple_of(first, 32), rows), slice(None))
            total = part[view].astype(F32)
            for ref in landed:
                total = total + ref[...].astype(F32)
            part[view] = total.astype(BF16)

        def fold(which):
            to_mate(which).wait_recv()
            add(which, mine, lane_half, l3.at[y, which])

        def near(which, d, land, index, target, narrow):
            if narrow:
                ref = piece(which, mine + d * lane_quarter, lane_quarter)
            else:
                ref = piece(which, mine, lane_half)
            return remote(ref, land, base + index, target)

        sign = (-1, 1)

        def first_b(k, d):
            return near(pair(k, 2), d, lb1.at[y, k, d], 16 + 4 * k + d, at(0, sign[d]), True)

        def second_b(k, d):
            return near(pair(k, sign[d]), d, lb2.at[y, k, d], 18 + 4 * k + d, at(0, sign[d]), False)

        def first_a(d):
            return near(pair(2, 0), d, la1.at[y, d], 32 + d, at(sign[d], 0), True)

        def second_a(d):
            return near(pair(sign[d], 0), d, la2.at[y, d], 34 + d, at(sign[d], 0), False)

        def r1(k):
            fold(pair(k, 2))
            for d in range(2):
                start(lambda d=d: first_b(k, d))

        def r2(k):
            for d in range(2):
                fold(pair(k, sign[d]))
                first_b(k, d).wait_recv()
                add(pair(k, sign[d]), mine + d * lane_quarter, lane_quarter, lb1.at[y, k, d])
                start(lambda d=d: second_b(k, d))

        def r3(k):
            fold(pair(k, 0))
            for d in range(2):
                second_b(k, d).wait_recv()
            add(pair(k, 0), mine, lane_half, lb2.at[y, k, 0], lb2.at[y, k, 1])
            if k == 2:
                for d in range(2):
                    start(lambda d=d: first_a(d))
            if k in (1, 3):
                d = 0 if k == 3 else 1
                first_a(d).wait_recv()
                add(pair(sign[d], 0), mine + d * lane_quarter, lane_quarter, la1.at[y, d])
                start(lambda: second_a(d))

        def last():
            def make(first, tile):
                ref = part.at[y, tile, pl.ds(pl.multiple_of(first, 32), lane_half), :]
                return remote(ref, l0.at[y], base + 36, (mate, my))

            for d in range(2):
                second_a(d).wait_recv()
            add(pair(0, 0), mine, lane_half, la2.at[y, 0], la2.at[y, 1])
            start(lambda: make(mine, mate))
            make(mine, mate).wait_recv()

        order = (2, 3, 1, 0)
        events = [functools.partial(r1, k) for k in order]
        events += [functools.partial(r2, k) for k in order]
        events += [functools.partial(r3, k) for k in order]
        return to_mate, events, last

    def outs(y, hbm, index):
        mine, other = c * lane_half, (1 - c) * lane_half
        near_out = pltpu.make_async_copy(
            part.at[y, me, pl.ds(pl.multiple_of(mine, 32), lane_half), :],
            hbm.at[pl.ds(pl.multiple_of(mine, 32), lane_half), :],
            loc.at[index],
        )
        far_out = pltpu.make_async_copy(
            l0.at[y], hbm.at[pl.ds(pl.multiple_of(other, 32), lane_half), :], loc.at[index + 1]
        )
        return near_out, far_out

    k0, k1, k_events, k_end = gather(kall, 0)
    v0, v1, v_events, v_end = gather(vall, 40)
    v_mate, dv_events, dv_last = reduce(0, 80)
    k_mate, dk_events, dk_last = reduce(1, 120)

    def scheduled(step, table):
        for moment, event in table:
            pl.when(step == moment)(event)

    k_in.wait()
    k0()
    gate_tanh = jnp.tanh(jnp.full((8, HEAD), gate[0], F32))
    tanh_row = jnp.broadcast_to(gate_tanh[0:1, 0:1], (span_len, HEAD))
    gacc[...] = jnp.zeros((8, HEAD), F32)
    k1()
    q_in.wait()
    c_in.wait()
    qs[spans] = jnp.zeros((heads * span_len, HEAD), BF16)
    gs[spans] = jnp.zeros((heads * span_len, HEAD), BF16)

    def lay_out(s, carry):
        rows = pl.ds(pl.multiple_of(s * span_len, span_len), span_len)
        for h in range(heads):
            cols = slice(h * HEAD, (h + 1) * HEAD)
            qs[s, h * span_len : (h + 1) * span_len, :] = qv[rows, cols]
            gs[s, h * span_len : (h + 1) * span_len, :] = (
                tanh_row * cv[rows, cols].astype(F32)
            ).astype(BF16)
        return carry

    lax.fori_loop(0, spans, lay_out, 0)
    v_in.wait()
    for event in k_events:
        event()
    v0()
    k_end()
    v1()

    def soften(s, carry):
        scores = nt(qs[s], kall[tiles[s]])
        top = jnp.max(scores, axis=1, keepdims=True)
        expo = jnp.exp((scores - top) * scale)
        inv = 1.0 / jnp.sum(expo, axis=1, keepdims=True)
        probs[s] = (expo * inv).astype(BF16)
        scheduled(s, zip((8, 10, 12, 13, 18, 20, 23, 25, 28, 30), v_events[:10]))
        return carry

    lax.fori_loop(0, spans, soften, 0)

    def tile_sum(rows, weights, tile):
        s0, s1 = slots[0, tile], slots[1, tile]
        cap = spans - 1
        return tn(rows[s0], weights[jnp.minimum(s0, cap)]) + tn(
            rows[s1], weights[jnp.minimum(s1, cap)]
        )

    def value_part(p, carry):
        for i in range(2):
            part[0, 2 * p + i] = tile_sum(gs, probs, 2 * p + i).astype(BF16)
        v_mate(p).start()
        scheduled(p, zip((1, 4, 6, 9, 12), v_events[10:]))
        return carry

    lax.fori_loop(0, spans // 2, value_part, 0)
    v_end()

    def backward(s, carry):
        rows = pl.ds(pl.multiple_of(s * span_len, span_len), span_len)
        values, weights, grads = vall[tiles[s]], probs[s], gs[s]
        attn = nn(weights, values).astype(BF16)
        attn_f = attn.astype(F32)
        delta = jnp.sum(grads.astype(F32) * attn_f, axis=1, keepdims=True)
        dscore = (weights.astype(F32) * (nt(grads, values) - delta) * scale).astype(BF16)
        probs[s] = dscore
        dq = nn(dscore, kall[tiles[s]]).astype(BF16)
        total = jnp.zeros((span_len, HEAD), F32)
        for h in range(heads):
            cols = slice(h * HEAD, (h + 1) * HEAD)
            block = slice(h * span_len, (h + 1) * span_len)
            qv[rows, cols] = dq[block]
            total = total + cv[rows, cols].astype(F32) * attn_f[block]
            cv[rows, cols] = (tanh_row * attn_f[block]).astype(BF16)
        gacc[...] += sum(total[8 * i : 8 * i + 8] for i in range(span_len // 8))
        scheduled(s, zip((0, 1, 2, 3, 14, 18, 22, 26), dv_events[:8]))
        return carry

    lax.fori_loop(0, spans, backward, 0)
    att_out = pltpu.make_async_copy(cv, att_hbm, loc.at[4])
    dq_out = pltpu.make_async_copy(qv, dq_hbm, loc.at[5])
    att_out.start()
    dq_out.start()

    def key_part(p, carry):
        for i in range(2):
            part[1, 2 * p + i] = tile_sum(qs, probs, 2 * p + i).astype(BF16)
        k_mate(p).start()
        scheduled(p, zip((2, 5, 8, 12), dv_events[8:]))
        return carry

    lax.fori_loop(0, spans // 2, key_part, 0)

    def exchange(stage, own, count, targets, base):
        for d, target in enumerate(targets):
            start(
                lambda d=d, target=target: remote(
                    gland.at[stage, own], gland.at[stage, own], base + d, target
                )
            )

    def settle(stage, count, targets, base):
        for d, target in enumerate(targets):
            remote(gland.at[stage, 0], gland.at[stage, 0], base + d, target).wait_recv()
        total = gland[stage, 0]
        for i in range(1, count):
            total = total + gland[stage, i]
        return total

    rings = (
        (c, 2, [(mate, my)]),
        (z, RING, [(8 * wrap(z + d) + 2 * x + c, my) for d in range(1, RING)]),
        (x, RING, [(8 * z + 2 * wrap(x + d) + c, my) for d in range(1, RING)]),
        (my, RING, [(me, wrap(my + d)) for d in range(1, RING)]),
    )
    gate_base = 160

    def gate_begin(stage, value):
        own, count, targets = rings[stage]
        gland[stage, own] = value
        exchange(stage, own, count, targets, gate_base + 3 * stage)

    def gate_end(stage):
        own, count, targets = rings[stage]
        return settle(stage, count, targets, gate_base + 3 * stage)

    gate_begin(0, gacc[...])
    for event in dk_events[:4]:
        event()
    dv_last()
    dv_outs = outs(0, dv_hbm, 6)
    for copy in dv_outs:
        copy.start()
    for event in dk_events[4:8]:
        event()
    gate_begin(1, gate_end(0))
    dk_events[8]()
    gate_begin(2, gate_end(1))
    dk_events[9]()
    dk_events[10]()
    gate_begin(3, gate_end(2))
    dk_events[11]()
    dk_last()
    dk_outs = outs(1, dk_hbm, 8)
    for copy in dk_outs:
        copy.start()
    grand = jnp.sum(gate_end(3))
    slope = (1.0 - gate_tanh * gate_tanh) * grand / math.sqrt(total_elems)
    gate_out[...] = slope

    for make in started:
        make().wait_send()

    def drain(p, carry):
        v_mate(p).wait_send()
        k_mate(p).wait_send()
        return carry

    lax.fori_loop(0, spans // 2, drain, 0)
    for copy in (att_out, dq_out) + dv_outs + dk_outs:
        copy.wait()


def body(queries, image_keys, image_values, span_tiles, gate_logit, cotangent):
    tok_count, columns = queries.shape
    spans = span_tiles.shape[0]
    span_len = tok_count // spans
    heads = columns // HEAD
    image_len = image_keys.shape[1]
    tile_count = lax.axis_size("seq")
    total_elems = tok_count * tile_count * columns * lax.axis_size("mp")
    owners = span_tiles[:, 0]
    numbers = jnp.arange(spans, dtype=jnp.int32)[:, None]
    hits = owners[:, None] == jnp.arange(tile_count, dtype=jnp.int32)[None, :]
    first = jnp.min(jnp.where(hits, numbers, spans), axis=0)
    final = jnp.max(jnp.where(hits, numbers, -1), axis=0)
    slots = jnp.stack([first, jnp.where(final > first, final, spans)])
    smem = pl.BlockSpec(memory_space=pltpu.SMEM)
    hbm = pl.BlockSpec(memory_space=pl.ANY)
    sizes = (spans, span_len, heads, image_len, total_elems)
    rows = heads * span_len
    kv = (tile_count, image_len, HEAD)
    att, dq, dk, dv, gate = pl.pallas_call(
        functools.partial(kernel, sizes),
        out_shape=(
            jax.ShapeDtypeStruct(queries.shape, BF16),
            jax.ShapeDtypeStruct(queries.shape, BF16),
            jax.ShapeDtypeStruct((HEAD, image_len), BF16),
            jax.ShapeDtypeStruct((HEAD, image_len), BF16),
            jax.ShapeDtypeStruct((8, HEAD), F32),
        ),
        in_specs=[smem, smem, smem, hbm, hbm, hbm, hbm],
        out_specs=(hbm, hbm, hbm, hbm, pl.BlockSpec(memory_space=pltpu.VMEM)),
        scratch_shapes=[
            pltpu.VMEM(kv, BF16),
            pltpu.VMEM(kv, BF16),
            pltpu.VMEM((spans, rows, image_len), BF16),
            pltpu.VMEM(queries.shape, BF16),
            pltpu.VMEM(queries.shape, BF16),
            pltpu.VMEM((spans + 1, rows, HEAD), BF16),
            pltpu.VMEM((spans + 1, rows, HEAD), BF16),
            pltpu.VMEM((2, tile_count, HEAD, image_len), BF16),
            pltpu.VMEM((2, tile_count // 2, 2, HEAD // 2, image_len), BF16),
            pltpu.VMEM((2, RING, 2, 2, HEAD // 4, image_len), BF16),
            pltpu.VMEM((2, RING, 2, 2, HEAD // 2, image_len), BF16),
            pltpu.VMEM((2, 2, 2, HEAD // 4, image_len), BF16),
            pltpu.VMEM((2, 2, 2, HEAD // 2, image_len), BF16),
            pltpu.VMEM((2, HEAD // 2, image_len), BF16),
            pltpu.VMEM((8, HEAD), F32),
            pltpu.VMEM((4, RING, 8, HEAD), F32),
            pltpu.SemaphoreType.DMA((172,)),
            pltpu.SemaphoreType.DMA((172,)),
            pltpu.SemaphoreType.DMA((10,)),
        ],
        compiler_params=pltpu.CompilerParams(
            collective_id=0, has_side_effects=True, vmem_limit_bytes=67043328
        ),
        name="cross_attention",
    )(owners, slots, gate_logit, queries, image_keys, image_values, cotangent)
    return (att, dq, dk.T[None], dv.T[None], gate[0, :1])


def solution(mesh):
    placed = (
        P("seq", "mp"),
        P("seq", None, "mp"),
        P("seq", None, "mp"),
        P("seq", None),
        P(),
        P("seq", "mp"),
    )
    return jax.shard_map(
        body,
        mesh=mesh,
        in_specs=placed,
        out_specs=(P("seq", "mp"), P("seq", "mp"), P("seq", None, "mp"), P("seq", None, "mp"), P()),
        check_vma=False,
    )
```

```python
import functools
import math

import jax
import jax.numpy as jnp
from jax import lax
from jax.experimental import pallas as pl
from jax.experimental.pallas import tpu as pltpu
from jax.sharding import PartitionSpec as P

HEAD = 128
RING = 4
LOG2E = 1.4426950408889634
MESH = pl.DeviceIdType.MESH
F32 = jnp.float32
BF16 = jnp.bfloat16


def nt(left, right):
    return lax.dot_general(left, right, (((1,), (1,)), ((), ())), preferred_element_type=F32)


def nn(left, right):
    return lax.dot_general(left, right, (((1,), (0,)), ((), ())), preferred_element_type=F32)


def tn(left, right):
    return lax.dot_general(left, right, (((0,), (0,)), ((), ())), preferred_element_type=F32)


def wrap(value):
    return lax.rem(value + RING, RING)


def kernel(
    sizes,
    tiles,
    gate,
    q_hbm,
    k_hbm,
    v_hbm,
    c_hbm,
    att_hbm,
    dq_hbm,
    dk_hbm,
    dv_hbm,
    gate_out,
    kall,
    vall,
    probs,
    cs,
    qs,
    gs,
    alone,
    part,
    slots_v,
    slots,
    l3,
    lb1,
    lb2,
    la1,
    la2,
    l0,
    upright,
    wide_a,
    wide_b,
    thin_a,
    thin_b,
    mid_a,
    mid_b,
    gacc,
    gland,
    send,
    recv,
    loc,
    free,
):
    spans, span_len, heads, image_len, total_elems = sizes
    scale = 1.0 / math.sqrt(HEAD)
    me = lax.axis_index("seq")
    my = lax.axis_index("mp")
    z = lax.div(me, 8)
    x = lax.rem(lax.div(me, 2), RING)
    c = lax.rem(me, 2)
    mate = me + 1 - 2 * c
    a = z * (1 - c) + x * c
    b = x * (1 - c) + z * c
    stride_a = 4 - 3 * c
    stride_b = 1 + 3 * c

    def pair(da, db):
        return wrap(a + da) * stride_a + wrap(b + db) * stride_b

    def mate_pair(da, db):
        return wrap(b + da) * stride_b + wrap(a + db) * stride_a

    def at(da, db):
        return (2 * pair(da, db) + c, my)

    barrier = pltpu.get_barrier_semaphore()
    friends = [(mate, my)]
    for d in range(1, RING):
        friends.append((8 * wrap(z + d) + 2 * x + c, my))
        friends.append((8 * z + 2 * wrap(x + d) + c, my))
        friends.append((me, wrap(my + d)))
    for friend in friends:
        pl.semaphore_signal(barrier, inc=1, device_id=friend, device_id_type=MESH)

    def by_head(hbm, buf, index, out):
        copies = []
        for h in range(heads):
            flat_side = hbm.at[:, :, pl.ds(h * HEAD, HEAD)]
            head_side = buf.at[pl.ds(0, spans), pl.ds(h * span_len, span_len), :]
            src, dst = (head_side, flat_side) if out else (flat_side, head_side)
            copies.append(pltpu.make_async_copy(src, dst, loc.at[index + h]))
        return copies

    k_in = pltpu.make_async_copy(k_hbm, kall.at[pl.ds(me, 1)], loc.at[0])
    v_in = pltpu.make_async_copy(v_hbm, vall.at[pl.ds(me, 1)], loc.at[1])
    rows_in = by_head(q_hbm, qs, 4, False) + by_head(c_hbm, cs, 4 + heads, False)
    k_in.start()
    v_in.start()
    for copy in rows_in:
        copy.start()
    pl.semaphore_wait(barrier, len(friends))

    started = []

    def remote(src, dst, index, target):
        return pltpu.make_async_remote_copy(
            src_ref=src,
            dst_ref=dst,
            send_sem=send.at[index],
            recv_sem=recv.at[index],
            device_id=target,
            device_id_type=MESH,
        )

    def start(make):
        make().start()
        started.append(make)

    half = image_len // 2
    quarter = half // 2
    steps = (0, -1, 1, 2)

    def gather(buf, base):
        mine, other = c * half, (1 - c) * half

        def piece(which, first, rows):
            return buf.at[pl.ds(2 * which, 2), pl.ds(pl.multiple_of(first, 64), rows), :]

        def own_copy(first, tile, index):
            ref = buf.at[pl.ds(tile, 1), pl.ds(pl.multiple_of(first, 64), half), :]
            return remote(ref, ref, base + index, (mate, my))

        def moved(which, direction, index, target, narrow):
            if narrow:
                ref = piece(which, mine + direction * quarter, quarter)
            else:
                ref = piece(which, mine, half)
            return remote(ref, ref, base + index, target)

        def to_mate(k, kb):
            ref = piece(pair(steps[k], steps[kb]), mine, half)
            return remote(ref, ref, base + 24 + 4 * k + kb, (mate, my))

        def from_mate(k, kb):
            ref = piece(mate_pair(steps[k], steps[kb]), other, half)
            return remote(ref, ref, base + 24 + 4 * k + kb, (mate, my))

        sign = (1, -1)

        def lone(tile, index, target):
            ref = buf.at[pl.ds(tile, 1), pl.ds(pl.multiple_of(mine, 64), half), :]
            return remote(ref, ref, base + index, target)

        def lone_a(tile, d, second):
            return lone(tile, (40 if second else 2) + d, at(sign[d], 0))

        def lone_b(tile, d, second):
            return lone(tile, (42 if second else 8) + d, at(0, sign[d]))

        def e0():
            start(lambda: own_copy(other, me, 0))
            for d in range(2):
                start(lambda d=d: lone_a(me, d, False))
                start(lambda d=d: lone_b(me, d, False))
            start(lambda: own_copy(mine, me, 1))

        def send_b(k):
            for d in range(2):
                start(lambda d=d: moved(pair(steps[k], 0), d, 8 + 4 * k + d, at(0, sign[d]), False))

        def e1():
            own_copy(mine, mate, 0).wait_recv()
            for d in range(2):
                start(lambda d=d: lone_a(mate, d, True))
                start(lambda d=d: lone_b(mate, d, True))

        def e_a(d):
            lone_a(2 * pair(-sign[d], 0) + c, d, False).wait_recv()
            lone_a(2 * pair(-sign[d], 0) + 1 - c, d, True).wait_recv()
            start(lambda: moved(pair(-sign[d], 0), d, 4 + d, at(sign[d], 0), True))
            send_b(1 + d)
            start(lambda: to_mate(1 + d, 0))

        def e_aq():
            for d in range(2):
                moved(pair(2, 0), d, 4 + d, at(sign[d], 0), True).wait_recv()
            send_b(3)
            start(lambda: to_mate(3, 0))

        def e_b(k, d):
            if k == 0:
                lone_b(2 * pair(0, -sign[d]) + c, d, False).wait_recv()
                lone_b(2 * pair(0, -sign[d]) + 1 - c, d, True).wait_recv()
            else:
                moved(pair(steps[k], -sign[d]), d, 8 + 4 * k + d, at(0, sign[d]), False).wait_recv()
            start(
                lambda: moved(
                    pair(steps[k], -sign[d]), d, 10 + 4 * k + d, at(0, sign[d]), True
                )
            )
            start(lambda: to_mate(k, 1 + d))

        def e_bq(k):
            for d in range(2):
                moved(pair(steps[k], 2), d, 10 + 4 * k + d, at(0, sign[d]), True).wait_recv()
            start(lambda: to_mate(k, 3))

        def e_end():
            own_copy(other, mate, 1).wait_recv()
            for k in range(4):
                for kb in range(4):
                    if k or kb:
                        from_mate(k, kb).wait_recv()

        events = [
            lambda: e_a(0),
            lambda: e_a(1),
            lambda: e_b(0, 0),
            lambda: e_b(0, 1),
            e_aq,
            lambda: e_b(1, 0),
            lambda: e_b(1, 1),
            lambda: e_b(2, 0),
            lambda: e_b(2, 1),
            lambda: e_bq(0),
            lambda: e_b(3, 0),
            lambda: e_b(3, 1),
            lambda: e_bq(1),
            lambda: e_bq(2),
            lambda: e_bq(3),
        ]
        return e0, e1, events, e_end

    lane_half = HEAD // 2
    lane_quarter = HEAD // 4

    def reduce(y, base):
        mine, other = c * lane_half, (1 - c) * lane_half

        def piece(which, first, rows):
            return part.at[y, pl.ds(2 * which, 2), pl.ds(pl.multiple_of(first, 32), rows), :]

        def landing(which):
            if y == 0:
                return l3.at[which]
            return probs.at[pl.ds(2 * which, 2), pl.ds(0, lane_half), :]

        def to_mate(which):
            return remote(piece(which, other, lane_half), landing(which), base + which, (mate, my))

        def add(which, first, rows, *landed):
            view = (y, pl.ds(2 * which, 2), pl.ds(pl.multiple_of(first, 32), rows), slice(None))
            total = part[view].astype(F32)
            for ref in landed:
                total = total + ref[...].astype(F32)
            part[view] = total.astype(BF16)

        def fold(which):
            to_mate(which).wait_recv()
            add(which, mine, lane_half, landing(which))

        def near(which, d, land, index, target, narrow):
            if narrow:
                ref = piece(which, mine + d * lane_quarter, lane_quarter)
            else:
                ref = piece(which, mine, lane_half)
            return remote(ref, land, base + index, target)

        sign = (-1, 1)

        def first_b(k, d):
            return near(pair(k, 2), d, lb1.at[y, k, d], 16 + 4 * k + d, at(0, sign[d]), True)

        def second_b(k, d):
            return near(pair(k, sign[d]), d, lb2.at[y, k, d], 18 + 4 * k + d, at(0, sign[d]), False)

        def first_a(d):
            return near(pair(2, 0), d, la1.at[y, d], 32 + d, at(sign[d], 0), True)

        def second_a(d):
            return near(pair(sign[d], 0), d, la2.at[y, d], 34 + d, at(sign[d], 0), False)

        def r1(k):
            fold(pair(k, 2))
            for d in range(2):
                start(lambda d=d: first_b(k, d))

        def r2(k):
            for d in range(2):
                fold(pair(k, sign[d]))
                first_b(k, d).wait_recv()
                add(pair(k, sign[d]), mine + d * lane_quarter, lane_quarter, lb1.at[y, k, d])
                start(lambda d=d: second_b(k, d))

        def r3(k):
            fold(pair(k, 0))
            for d in range(2):
                second_b(k, d).wait_recv()
            add(pair(k, 0), mine, lane_half, lb2.at[y, k, 0], lb2.at[y, k, 1])
            if k == 2:
                for d in range(2):
                    start(lambda d=d: first_a(d))
            if k in (1, 3):
                d = 0 if k == 3 else 1
                first_a(d).wait_recv()
                add(pair(sign[d], 0), mine + d * lane_quarter, lane_quarter, la1.at[y, d])
                start(lambda: second_a(d))

        def last():
            def make(first, tile):
                ref = part.at[y, tile, pl.ds(pl.multiple_of(first, 32), lane_half), :]
                return remote(ref, l0.at[y], base + 36, (mate, my))

            for d in range(2):
                second_a(d).wait_recv()
            add(pair(0, 0), mine, lane_half, la2.at[y, 0], la2.at[y, 1])
            start(lambda: make(mine, mate))
            make(mine, mate).wait_recv()

        order = (2, 3, 1, 0)
        events = [functools.partial(r1, k) for k in order]
        events += [functools.partial(r2, k) for k in order]
        events += [functools.partial(r3, k) for k in order]
        return to_mate, events, last

    def finish(y, hbm, index):
        mine, other = c * lane_half, (1 - c) * lane_half
        mid_a[pl.ds(pl.multiple_of(mine, 32), lane_half), :] = part[
            y, me, pl.ds(pl.multiple_of(mine, 32), lane_half), :
        ]
        mid_a[pl.ds(pl.multiple_of(other, 32), lane_half), :] = l0[y]
        upright[y] = mid_a[0:HEAD, :].T
        copy = pltpu.make_async_copy(upright.at[pl.ds(y, 1)], hbm, loc.at[index])
        copy.start()
        return copy

    k0, k1, k_events, k_end = gather(kall, 0)
    v0, v1, v_events, v_end = gather(vall, 44)
    v_mate, dv_events, dv_last = reduce(0, 88)
    k_mate, dk_events, dk_last = reduce(1, 128)

    def run(step, total, cuts):
        low = 0
        for high, events in cuts:
            if high > low:
                lax.fori_loop(low, high, step, 0)
            low = high
            for event in events:
                event()
        if low < total:
            lax.fori_loop(low, total, step, 0)

    def flush():
        for make in started:
            make().wait_send()
        started.clear()

    rings = (
        (c, [(mate, my)]),
        (z, [(8 * wrap(z + d) + 2 * x + c, my) for d in range(1, RING)]),
        (x, [(8 * z + 2 * wrap(x + d) + c, my) for d in range(1, RING)]),
        (my, [(me, wrap(my + d)) for d in range(1, RING)]),
    )
    gate_base = 168

    def gate_copy(stage, d):
        own, targets = rings[stage]
        ref = gland.at[stage, own]
        return remote(ref, ref, gate_base + 3 * stage + d, targets[d])

    def gate_begin(stage, value):
        own, targets = rings[stage]
        gland[stage, own] = value
        for d in range(len(targets)):
            start(lambda d=d: gate_copy(stage, d))

    def gate_end(stage):
        own, targets = rings[stage]
        for d in range(len(targets)):
            gate_copy(stage, d).wait_recv()
        total = gland[stage, 0]
        for i in range(1, len(targets) + 1):
            total = total + gland[stage, i]
        return total

    k_in.wait()
    k0()
    lane = lax.broadcasted_iota(jnp.int32, (1, HEAD), 1)
    first = final = jnp.full((1, HEAD), spans, jnp.int32)
    for s in range(spans):
        hit = lane == tiles[s]
        final = jnp.where(hit, s, final)
        first = jnp.where(hit & (first == spans), s, first)
    slots_v[0:1, :] = first
    slots_v[1:2, :] = jnp.where(final > first, final, spans)
    slots_copy = pltpu.make_async_copy(slots_v, slots, loc.at[2])
    slots_copy.start()
    gate_tanh = jnp.tanh(jnp.full((8, HEAD), gate[0], F32))
    tanh_row = jnp.broadcast_to(gate_tanh[0:1, 0:1], (heads * span_len, HEAD))
    gacc[...] = jnp.zeros((8, HEAD), F32)
    alone[spans] = jnp.zeros((HEAD, image_len), BF16)
    qs[spans] = jnp.zeros((heads * span_len, HEAD), BF16)
    mid_b[...] = jnp.zeros((heads * span_len, image_len), BF16)
    k1()
    v_in.wait()
    v0()
    for event in k_events[:9]:
        event()
    for copy in rows_in:
        copy.wait()

    def gated(s, carry):
        gs[s] = (tanh_row * cs[s].astype(F32)).astype(BF16)
        return carry

    lax.fori_loop(0, spans, gated, 0)
    for event in k_events[9:12]:
        event()
    v1()
    for event in k_events[12:]:
        event()
    k_end()

    cap = spans - 1

    def score(s, wide):
        wide[...] = nt(qs[s], kall[tiles[s]])

    def soften(s, wide, mid):
        scores = wide[...]
        top = jnp.max(scores, axis=1, keepdims=True)
        expo = jnp.exp2((scores - top) * (scale * LOG2E))
        inv = 1.0 / jnp.sum(expo, axis=1, keepdims=True)
        weights = (expo * inv).astype(BF16)
        probs[s] = weights
        mid[...] = weights

    def before(i):
        return jnp.where(i == 0, spans, 2 * i - 1)

    def value_alone(s, mid):
        alone[s] = tn(gs[jnp.minimum(s, cap)], mid[...]).astype(BF16)

    def soften_two(i, carry):
        score(2 * i + 1, wide_b)
        value_alone(before(i), mid_b)
        soften(2 * i, wide_a, mid_a)
        score(jnp.minimum(2 * i + 2, cap), wide_a)
        value_alone(2 * i, mid_a)
        soften(2 * i + 1, wide_b, mid_b)
        return carry

    score(0, wide_a)
    run(
        soften_two,
        spans // 2,
        (
            (4, v_events[:4]),
            (9, v_events[4:5]),
            (13, v_events[5:9]),
            (16, v_events[9:10]),
        ),
    )

    value_alone(cap, mid_b)
    mid_b[...] = jnp.zeros((heads * span_len, image_len), BF16)

    slots_copy.wait()

    def partials(y, mate_copy, cuts):
        def add_pair(which):
            for i in range(2):
                tile = 2 * which + i
                both = alone[slots[0, tile]].astype(F32) + alone[slots[1, tile]].astype(F32)
                part[y, tile] = both.astype(BF16)
            mate_copy(which).start()

        def along_x(i, carry):
            add_pair(RING * wrap(z + 2) + wrap(x + i))
            return carry

        def along_z(i, carry):
            add_pair(RING * wrap(z + 3 + i) + wrap(x + 2))
            return carry

        def inner(u):
            def step(i, carry):
                add_pair(RING * wrap(z + u) + wrap(x + 3 + i))
                return carry

            return step

        loops = [(along_x, 4), (along_z, 3), (inner(3), 3), (inner(1), 3), (inner(0), 3)]
        for (step, count), events in zip(loops, cuts):
            lax.fori_loop(0, count, step, 0)
            for event in events:
                event()

    partials(
        0,
        v_mate,
        (v_events[10:12], dv_events[:2], dv_events[2:4] + v_events[12:13], v_events[13:14], ()),
    )
    v_events[14]()
    v_end()

    def spread(s, wide, thin):
        values = vall[tiles[s]]
        wide[...] = nt(gs[s], values)
        thin[...] = nn(probs[s], values).astype(BF16)

    def backward(s, wide, thin, mid):
        attn_f = thin[...].astype(F32)
        delta = jnp.sum(gs[s].astype(F32) * attn_f, axis=1, keepdims=True)
        mid[...] = (probs[s].astype(F32) * (wide[...] - delta) * scale).astype(BF16)
        product = cs[s].astype(F32) * attn_f
        cs[s] = thin[...]
        gacc[...] += sum(product[8 * i : 8 * i + 8] for i in range(heads * span_len // 8))

    def key_alone(s, mid):
        dscore = mid[...]
        alone[s] = tn(qs[s], dscore).astype(BF16)
        qs[s] = nn(dscore, kall[tiles[jnp.minimum(s, cap)]]).astype(BF16)

    def backward_two(i, carry):
        spread(2 * i + 1, wide_b, thin_b)
        key_alone(before(i), mid_b)
        backward(2 * i, wide_a, thin_a, mid_a)
        spread(jnp.minimum(2 * i + 2, cap), wide_a, thin_a)
        key_alone(2 * i, mid_a)
        backward(2 * i + 1, wide_b, thin_b, mid_b)
        return carry

    spread(0, wide_a, thin_a)
    run(
        backward_two,
        spans // 2,
        (
            (2, dv_events[4:6]),
            (4, dv_events[6:8]),
            (7, dv_events[8:9]),
            (11, dv_events[9:11]),
            (14, dv_events[11:12]),
            (16, ()),
        ),
    )
    pl.semaphore_signal(free, inc=1, device_id=(mate, my), device_id_type=MESH)
    gate_begin(0, gacc[...])
    key_alone(cap, mid_b)
    rows_out = by_head(att_hbm, cs, 4, True) + by_head(dq_hbm, qs, 4 + heads, True)
    for copy in rows_out:
        copy.start()

    pl.semaphore_wait(free, 1)
    dv_out = []

    def dv_done():
        dv_last()
        dv_out.append(finish(0, dv_hbm, 2))

    partials(
        1,
        k_mate,
        (
            [dv_done],
            [lambda: gate_begin(1, gate_end(0))] + dk_events[:2],
            dk_events[2:4],
            [lambda: gate_begin(2, gate_end(1))],
            [],
        ),
    )
    flush()
    for event in dk_events[4:6]:
        event()
    gate_begin(3, gate_end(2))
    for event in dk_events[6:8]:
        event()
    dk_events[8]()
    dk_events[9]()
    grand = jnp.sum(gate_end(3))
    slope = (1.0 - gate_tanh * gate_tanh) * grand / math.sqrt(total_elems)
    gate_out[0] = slope[0, 0]
    for event in dk_events[10:]:
        event()
    flush()

    def drain(p, carry):
        v_mate(p).wait_send()
        k_mate(p).wait_send()
        return carry

    lax.fori_loop(0, spans // 2, drain, 0)
    dk_last()
    dk_out = finish(1, dk_hbm, 3)
    flush()
    for copy in rows_out + [dk_out] + dv_out:
        copy.wait()


def body(queries, image_keys, image_values, span_tiles, gate_logit, cotangent):
    tok_count, columns = queries.shape
    spans = span_tiles.shape[0]
    span_len = tok_count // spans
    heads = columns // HEAD
    image_len = image_keys.shape[1]
    tile_count = lax.axis_size("seq")
    total_elems = tok_count * tile_count * columns * lax.axis_size("mp")
    smem = pl.BlockSpec(memory_space=pltpu.SMEM)
    hbm = pl.BlockSpec(memory_space=pl.ANY)
    sizes = (spans, span_len, heads, image_len, total_elems)
    rows = heads * span_len
    kv = (tile_count, image_len, HEAD)
    by_span = (spans, span_len, columns)
    att, dq, dk, dv, gate = pl.pallas_call(
        functools.partial(kernel, sizes),
        out_shape=(
            jax.ShapeDtypeStruct(by_span, BF16),
            jax.ShapeDtypeStruct(by_span, BF16),
            jax.ShapeDtypeStruct(image_keys.shape, BF16),
            jax.ShapeDtypeStruct(image_values.shape, BF16),
            jax.ShapeDtypeStruct((1,), F32),
        ),
        in_specs=[smem, smem, hbm, hbm, hbm, hbm],
        out_specs=(hbm, hbm, hbm, hbm, smem),
        scratch_shapes=[
            pltpu.VMEM(kv, BF16),
            pltpu.VMEM(kv, BF16),
            pltpu.VMEM((spans, rows, image_len), BF16),
            pltpu.VMEM((spans, rows, HEAD), BF16),
            pltpu.VMEM((spans + 1, rows, HEAD), BF16),
            pltpu.VMEM((spans, rows, HEAD), BF16),
            pltpu.VMEM((spans + 1, HEAD, image_len), BF16),
            pltpu.VMEM((2, tile_count, HEAD, image_len), BF16),
            pltpu.VMEM((2, HEAD), jnp.int32),
            pltpu.SMEM((2, HEAD), jnp.int32),
            pltpu.VMEM((tile_count // 2, 2, HEAD // 2, image_len), BF16),
            pltpu.VMEM((2, RING, 2, 2, HEAD // 4, image_len), BF16),
            pltpu.VMEM((2, RING, 2, 2, HEAD // 2, image_len), BF16),
            pltpu.VMEM((2, 2, 2, HEAD // 4, image_len), BF16),
            pltpu.VMEM((2, 2, 2, HEAD // 2, image_len), BF16),
            pltpu.VMEM((2, HEAD // 2, image_len), BF16),
            pltpu.VMEM((2, image_len, HEAD), BF16),
            pltpu.VMEM((rows, image_len), F32),
            pltpu.VMEM((rows, image_len), F32),
            pltpu.VMEM((rows, HEAD), BF16),
            pltpu.VMEM((rows, HEAD), BF16),
            pltpu.VMEM((rows, image_len), BF16),
            pltpu.VMEM((rows, image_len), BF16),
            pltpu.VMEM((8, HEAD), F32),
            pltpu.VMEM((4, RING, 8, HEAD), F32),
            pltpu.SemaphoreType.DMA((180,)),
            pltpu.SemaphoreType.DMA((180,)),
            pltpu.SemaphoreType.DMA((4 + 2 * heads,)),
            pltpu.SemaphoreType.REGULAR,
        ],
        compiler_params=pltpu.CompilerParams(
            collective_id=0, has_side_effects=True, vmem_limit_bytes=67043328
        ),
        name="cross_attention",
    )(
        span_tiles.reshape(spans),
        gate_logit,
        queries.reshape(by_span),
        image_keys,
        image_values,
        cotangent.reshape(by_span),
    )
    gate_tanh = jnp.tanh(gate_logit[0])
    attended = (gate_tanh * att.reshape(queries.shape).astype(F32)).astype(BF16)
    return (attended, dq.reshape(queries.shape), dk, dv, gate)


def solution(mesh):
    placed = (
        P("seq", "mp"),
        P("seq", None, "mp"),
        P("seq", None, "mp"),
        P("seq", None),
        P(),
        P("seq", "mp"),
    )
    return jax.shard_map(
        body,
        mesh=mesh,
        in_specs=placed,
        out_specs=(P("seq", "mp"), P("seq", "mp"), P("seq", None, "mp"), P("seq", None, "mp"), P()),
        check_vma=False,
    )
```

```python
import functools
import math

import jax
import jax.numpy as jnp
from jax import lax
from jax.experimental import pallas as pl
from jax.experimental.pallas import tpu as pltpu
from jax.sharding import PartitionSpec as P

HEAD = 128
RING = 4
LOG2E = 1.4426950408889634
MESH = pl.DeviceIdType.MESH
F32 = jnp.float32
BF16 = jnp.bfloat16


def nt(left, right):
    return lax.dot_general(left, right, (((1,), (1,)), ((), ())), preferred_element_type=F32)


def nn(left, right):
    return lax.dot_general(left, right, (((1,), (0,)), ((), ())), preferred_element_type=F32)


def tn(left, right):
    return lax.dot_general(left, right, (((0,), (0,)), ((), ())), preferred_element_type=F32)


def wrap(value):
    return lax.rem(value + RING, RING)


def kernel(
    sizes,
    tiles,
    gate,
    q_hbm,
    k_hbm,
    v_hbm,
    c_hbm,
    att_hbm,
    dq_hbm,
    dk_hbm,
    dv_hbm,
    gate_out,
    kall,
    vall,
    probs,
    cs,
    qs,
    gs,
    alone,
    part,
    slots_v,
    slots,
    l3,
    lb1,
    lb2,
    la1,
    la2,
    l0,
    upright,
    wide_a,
    wide_b,
    thin_a,
    thin_b,
    mid_a,
    mid_b,
    gacc,
    gland,
    send,
    recv,
    loc,
    free,
):
    spans, span_len, heads, image_len, total_elems = sizes
    scale = 1.0 / math.sqrt(HEAD)
    me = lax.axis_index("seq")
    my = lax.axis_index("mp")
    z = lax.div(me, 8)
    x = lax.rem(lax.div(me, 2), RING)
    c = lax.rem(me, 2)
    mate = me + 1 - 2 * c
    a = z * (1 - c) + x * c
    b = x * (1 - c) + z * c
    stride_a = 4 - 3 * c
    stride_b = 1 + 3 * c

    def pair(da, db):
        return wrap(a + da) * stride_a + wrap(b + db) * stride_b

    def mate_pair(da, db):
        return wrap(b + da) * stride_b + wrap(a + db) * stride_a

    def at(da, db):
        return (2 * pair(da, db) + c, my)

    barrier = pltpu.get_barrier_semaphore()
    friends = [(mate, my)]
    for d in range(1, RING):
        friends.append((8 * wrap(z + d) + 2 * x + c, my))
        friends.append((8 * z + 2 * wrap(x + d) + c, my))
        friends.append((me, wrap(my + d)))
    for friend in friends:
        pl.semaphore_signal(barrier, inc=1, device_id=friend, device_id_type=MESH)

    def by_head(hbm, buf, index, out):
        copies = []
        for h in range(heads):
            flat_side = hbm.at[:, :, pl.ds(h * HEAD, HEAD)]
            head_side = buf.at[pl.ds(0, spans), pl.ds(h * span_len, span_len), :]
            src, dst = (head_side, flat_side) if out else (flat_side, head_side)
            copies.append(pltpu.make_async_copy(src, dst, loc.at[index + h]))
        return copies

    k_in = pltpu.make_async_copy(k_hbm, kall.at[pl.ds(me, 1)], loc.at[0])
    v_in = pltpu.make_async_copy(v_hbm, vall.at[pl.ds(me, 1)], loc.at[1])
    rows_in = by_head(q_hbm, qs, 4, False) + by_head(c_hbm, cs, 4 + heads, False)
    k_in.start()
    v_in.start()
    for copy in rows_in:
        copy.start()
    pl.semaphore_wait(barrier, len(friends))

    started = []

    def remote(src, dst, index, target):
        return pltpu.make_async_remote_copy(
            src_ref=src,
            dst_ref=dst,
            send_sem=send.at[index],
            recv_sem=recv.at[index],
            device_id=target,
            device_id_type=MESH,
        )

    def start(make):
        make().start()
        started.append(make)

    half = image_len // 2
    quarter = half // 2
    steps = (0, -1, 1, 2)

    def gather(buf, base):
        mine, other = c * half, (1 - c) * half

        def piece(which, first, rows):
            return buf.at[pl.ds(2 * which, 2), pl.ds(pl.multiple_of(first, 64), rows), :]

        def own_copy(first, tile, index):
            ref = buf.at[pl.ds(tile, 1), pl.ds(pl.multiple_of(first, 64), half), :]
            return remote(ref, ref, base + index, (mate, my))

        def moved(which, direction, index, target, narrow):
            if narrow:
                ref = piece(which, mine + direction * quarter, quarter)
            else:
                ref = piece(which, mine, half)
            return remote(ref, ref, base + index, target)

        def to_mate(k, kb):
            ref = piece(pair(steps[k], steps[kb]), mine, half)
            return remote(ref, ref, base + 24 + 4 * k + kb, (mate, my))

        def from_mate(k, kb):
            ref = piece(mate_pair(steps[k], steps[kb]), other, half)
            return remote(ref, ref, base + 24 + 4 * k + kb, (mate, my))

        sign = (1, -1)

        def lone(tile, index, target):
            ref = buf.at[pl.ds(tile, 1), pl.ds(pl.multiple_of(mine, 64), half), :]
            return remote(ref, ref, base + index, target)

        def lone_a(tile, d, second):
            return lone(tile, (40 if second else 2) + d, at(sign[d], 0))

        def lone_b(tile, d, second):
            return lone(tile, (42 if second else 8) + d, at(0, sign[d]))

        def e0():
            start(lambda: own_copy(other, me, 0))
            for d in range(2):
                start(lambda d=d: lone_a(me, d, False))
                start(lambda d=d: lone_b(me, d, False))
            start(lambda: own_copy(mine, me, 1))

        def send_b(k):
            for d in range(2):
                start(lambda d=d: moved(pair(steps[k], 0), d, 8 + 4 * k + d, at(0, sign[d]), False))

        def e1():
            own_copy(mine, mate, 0).wait_recv()
            for d in range(2):
                start(lambda d=d: lone_a(mate, d, True))
                start(lambda d=d: lone_b(mate, d, True))

        def e_a(d):
            lone_a(2 * pair(-sign[d], 0) + c, d, False).wait_recv()
            lone_a(2 * pair(-sign[d], 0) + 1 - c, d, True).wait_recv()
            start(lambda: moved(pair(-sign[d], 0), d, 4 + d, at(sign[d], 0), True))
            send_b(1 + d)
            start(lambda: to_mate(1 + d, 0))

        def e_aq():
            for d in range(2):
                moved(pair(2, 0), d, 4 + d, at(sign[d], 0), True).wait_recv()
            send_b(3)
            start(lambda: to_mate(3, 0))

        def e_b(k, d):
            if k == 0:
                lone_b(2 * pair(0, -sign[d]) + c, d, False).wait_recv()
                lone_b(2 * pair(0, -sign[d]) + 1 - c, d, True).wait_recv()
            else:
                moved(pair(steps[k], -sign[d]), d, 8 + 4 * k + d, at(0, sign[d]), False).wait_recv()
            start(
                lambda: moved(
                    pair(steps[k], -sign[d]), d, 10 + 4 * k + d, at(0, sign[d]), True
                )
            )
            start(lambda: to_mate(k, 1 + d))

        def e_bq(k):
            for d in range(2):
                moved(pair(steps[k], 2), d, 10 + 4 * k + d, at(0, sign[d]), True).wait_recv()
            start(lambda: to_mate(k, 3))

        def e_end():
            own_copy(other, mate, 1).wait_recv()
            for k in range(4):
                for kb in range(4):
                    if k or kb:
                        from_mate(k, kb).wait_recv()

        events = [
            lambda: e_a(0),
            lambda: e_a(1),
            lambda: e_b(0, 0),
            lambda: e_b(0, 1),
            e_aq,
            lambda: e_b(1, 0),
            lambda: e_b(1, 1),
            lambda: e_b(2, 0),
            lambda: e_b(2, 1),
            lambda: e_bq(0),
            lambda: e_b(3, 0),
            lambda: e_b(3, 1),
            lambda: e_bq(1),
            lambda: e_bq(2),
            lambda: e_bq(3),
        ]
        return e0, e1, events, e_end

    lane_half = HEAD // 2
    lane_quarter = HEAD // 4

    def reduce(y, base):
        mine, other = c * lane_half, (1 - c) * lane_half

        def piece(which, first, rows):
            return part.at[y, pl.ds(2 * which, 2), pl.ds(pl.multiple_of(first, 32), rows), :]

        def landing(which):
            if y == 0:
                return l3.at[which]
            return probs.at[pl.ds(2 * which, 2), pl.ds(0, lane_half), :]

        def to_mate(which):
            return remote(piece(which, other, lane_half), landing(which), base + which, (mate, my))

        def add(which, first, rows, *landed):
            view = (y, pl.ds(2 * which, 2), pl.ds(pl.multiple_of(first, 32), rows), slice(None))
            total = part[view].astype(F32)
            for ref in landed:
                total = total + ref[...].astype(F32)
            part[view] = total.astype(BF16)

        def fold(which):
            to_mate(which).wait_recv()
            add(which, mine, lane_half, landing(which))

        def near(which, d, land, index, target, narrow):
            if narrow:
                ref = piece(which, mine + d * lane_quarter, lane_quarter)
            else:
                ref = piece(which, mine, lane_half)
            return remote(ref, land, base + index, target)

        sign = (-1, 1)

        def first_b(k, d):
            return near(pair(k, 2), d, lb1.at[y, k, d], 16 + 4 * k + d, at(0, sign[d]), True)

        def second_b(k, d):
            return near(pair(k, sign[d]), d, lb2.at[y, k, d], 18 + 4 * k + d, at(0, sign[d]), False)

        def first_a(d):
            return near(pair(2, 0), d, la1.at[y, d], 32 + d, at(sign[d], 0), True)

        def second_a(d):
            return near(pair(sign[d], 0), d, la2.at[y, d], 34 + d, at(sign[d], 0), False)

        def r1(k):
            fold(pair(k, 2))
            for d in range(2):
                start(lambda d=d: first_b(k, d))

        def r2(k):
            for d in range(2):
                fold(pair(k, sign[d]))
                first_b(k, d).wait_recv()
                add(pair(k, sign[d]), mine + d * lane_quarter, lane_quarter, lb1.at[y, k, d])
                start(lambda d=d: second_b(k, d))

        def r3(k):
            fold(pair(k, 0))
            for d in range(2):
                second_b(k, d).wait_recv()
            add(pair(k, 0), mine, lane_half, lb2.at[y, k, 0], lb2.at[y, k, 1])
            if k == 2:
                for d in range(2):
                    start(lambda d=d: first_a(d))
            if k in (1, 3):
                d = 0 if k == 3 else 1
                first_a(d).wait_recv()
                add(pair(sign[d], 0), mine + d * lane_quarter, lane_quarter, la1.at[y, d])
                start(lambda: second_a(d))

        def last():
            def make(first, tile):
                ref = part.at[y, tile, pl.ds(pl.multiple_of(first, 32), lane_half), :]
                return remote(ref, l0.at[y], base + 36, (mate, my))

            for d in range(2):
                second_a(d).wait_recv()
            add(pair(0, 0), mine, lane_half, la2.at[y, 0], la2.at[y, 1])
            start(lambda: make(mine, mate))
            make(mine, mate).wait_recv()

        order = (2, 3, 1, 0)
        events = [functools.partial(r1, k) for k in order]
        events += [functools.partial(r2, k) for k in order]
        events += [functools.partial(r3, k) for k in order]
        return to_mate, events, last

    def finish(y, hbm, index):
        mine, other = c * lane_half, (1 - c) * lane_half
        mid_a[pl.ds(pl.multiple_of(mine, 32), lane_half), :] = part[
            y, me, pl.ds(pl.multiple_of(mine, 32), lane_half), :
        ]
        mid_a[pl.ds(pl.multiple_of(other, 32), lane_half), :] = l0[y]
        upright[y] = mid_a[0:HEAD, :].T
        copy = pltpu.make_async_copy(upright.at[pl.ds(y, 1)], hbm, loc.at[index])
        copy.start()
        return copy

    k0, k1, k_events, k_end = gather(kall, 0)
    v0, v1, v_events, v_end = gather(vall, 44)
    v_mate, dv_events, dv_last = reduce(0, 88)
    k_mate, dk_events, dk_last = reduce(1, 128)

    def run(step, total, cuts):
        low = 0
        for high, events in cuts:
            if high > low:
                lax.fori_loop(low, high, step, 0)
            low = high
            for event in events:
                event()
        if low < total:
            lax.fori_loop(low, total, step, 0)

    def flush():
        for make in started:
            make().wait_send()
        started.clear()

    rings = (
        (c, [(mate, my)]),
        (z, [(8 * wrap(z + d) + 2 * x + c, my) for d in range(1, RING)]),
        (x, [(8 * z + 2 * wrap(x + d) + c, my) for d in range(1, RING)]),
        (my, [(me, wrap(my + d)) for d in range(1, RING)]),
    )
    gate_base = 168

    def gate_copy(stage, d):
        own, targets = rings[stage]
        ref = gland.at[stage, own]
        return remote(ref, ref, gate_base + 3 * stage + d, targets[d])

    def gate_begin(stage, value):
        own, targets = rings[stage]
        gland[stage, own] = value
        for d in range(len(targets)):
            start(lambda d=d: gate_copy(stage, d))

    def gate_end(stage):
        own, targets = rings[stage]
        for d in range(len(targets)):
            gate_copy(stage, d).wait_recv()
        total = gland[stage, 0]
        for i in range(1, len(targets) + 1):
            total = total + gland[stage, i]
        return total

    k_in.wait()
    k0()
    lane = lax.broadcasted_iota(jnp.int32, (1, HEAD), 1)
    first = final = jnp.full((1, HEAD), spans, jnp.int32)
    for s in range(spans):
        hit = lane == tiles[s]
        final = jnp.where(hit, s, final)
        first = jnp.where(hit & (first == spans), s, first)
    slots_v[0:1, :] = first
    slots_v[1:2, :] = jnp.where(final > first, final, spans)
    slots_copy = pltpu.make_async_copy(slots_v, slots, loc.at[2])
    slots_copy.start()
    gate_tanh = jnp.tanh(jnp.full((8, HEAD), gate[0], F32))
    tanh_row = jnp.broadcast_to(gate_tanh[0:1, 0:1], (heads * span_len, HEAD))
    gacc[...] = jnp.zeros((8, HEAD), F32)
    alone[spans] = jnp.zeros((HEAD, image_len), BF16)
    qs[spans] = jnp.zeros((heads * span_len, HEAD), BF16)
    mid_b[...] = jnp.zeros((heads * span_len, image_len), BF16)
    k1()
    v_in.wait()
    v0()
    for event in k_events[:9]:
        event()
    for copy in rows_in:
        copy.wait()

    def gated(s, carry):
        gs[s] = (tanh_row * cs[s].astype(F32)).astype(BF16)
        return carry

    lax.fori_loop(0, spans, gated, 0)
    for event in k_events[9:12]:
        event()
    v1()
    for event in k_events[12:]:
        event()
    k_end()

    cap = spans - 1

    def score(s, wide):
        wide[...] = nt(qs[s], kall[tiles[s]])

    def soften(s, wide, mid):
        scores = wide[...]
        top = jnp.max(scores, axis=1, keepdims=True)
        expo = jnp.exp2((scores - top) * (scale * LOG2E))
        inv = 1.0 / jnp.sum(expo, axis=1, keepdims=True)
        weights = (expo * inv).astype(BF16)
        probs[s] = weights
        mid[...] = weights

    def before(i):
        return jnp.where(i == 0, spans, 2 * i - 1)

    def value_alone(s, mid):
        alone[s] = tn(gs[jnp.minimum(s, cap)], mid[...]).astype(BF16)

    def soften_two(i, carry):
        score(2 * i + 1, wide_b)
        value_alone(before(i), mid_b)
        soften(2 * i, wide_a, mid_a)
        score(jnp.minimum(2 * i + 2, cap), wide_a)
        value_alone(2 * i, mid_a)
        soften(2 * i + 1, wide_b, mid_b)
        return carry

    score(0, wide_a)
    run(
        soften_two,
        spans // 2,
        (
            (4, v_events[:4]),
            (9, v_events[4:5]),
            (13, v_events[5:9]),
            (16, v_events[9:10]),
        ),
    )

    value_alone(cap, mid_b)
    mid_b[...] = jnp.zeros((heads * span_len, image_len), BF16)

    slots_copy.wait()

    def partials(y, mate_copy, cuts):
        def add_pair(which):
            for i in range(2):
                tile = 2 * which + i
                both = alone[slots[0, tile]].astype(F32) + alone[slots[1, tile]].astype(F32)
                part[y, tile] = both.astype(BF16)
            mate_copy(which).start()

        def along_x(i, carry):
            add_pair(RING * wrap(z + 2) + wrap(x + i))
            return carry

        def along_z(i, carry):
            add_pair(RING * wrap(z + 3 + i) + wrap(x + 2))
            return carry

        def inner(u):
            def step(i, carry):
                add_pair(RING * wrap(z + u) + wrap(x + 3 + i))
                return carry

            return step

        loops = [(along_x, 4), (along_z, 3), (inner(3), 3), (inner(1), 3), (inner(0), 3)]
        for (step, count), events in zip(loops, cuts):
            lax.fori_loop(0, count, step, 0)
            for event in events:
                event()

    partials(
        0,
        v_mate,
        (v_events[10:12], dv_events[:2], dv_events[2:4] + v_events[12:13], v_events[13:14], ()),
    )
    v_events[14]()
    v_end()

    def spread(s, wide, thin):
        values = vall[tiles[s]]
        wide[...] = nt(gs[s], values)
        thin[...] = nn(probs[s], values).astype(BF16)

    def backward(s, wide, thin, mid):
        attn_f = thin[...].astype(F32)
        delta = jnp.sum(gs[s].astype(F32) * attn_f, axis=1, keepdims=True)
        mid[...] = (probs[s].astype(F32) * (wide[...] - delta) * scale).astype(BF16)
        product = cs[s].astype(F32) * attn_f
        cs[s] = thin[...]
        gacc[...] += sum(product[8 * i : 8 * i + 8] for i in range(heads * span_len // 8))

    def key_alone(s, mid):
        dscore = mid[...]
        alone[s] = tn(qs[s], dscore).astype(BF16)
        qs[s] = nn(dscore, kall[tiles[jnp.minimum(s, cap)]]).astype(BF16)

    def backward_two(i, carry):
        spread(2 * i + 1, wide_b, thin_b)
        key_alone(before(i), mid_b)
        backward(2 * i, wide_a, thin_a, mid_a)
        spread(jnp.minimum(2 * i + 2, cap), wide_a, thin_a)
        key_alone(2 * i, mid_a)
        backward(2 * i + 1, wide_b, thin_b, mid_b)
        return carry

    spread(0, wide_a, thin_a)
    run(
        backward_two,
        spans // 2,
        (
            (2, dv_events[4:6]),
            (4, dv_events[6:8]),
            (7, dv_events[8:9]),
            (11, dv_events[9:11]),
            (14, dv_events[11:12]),
            (16, ()),
        ),
    )
    pl.semaphore_signal(free, inc=1, device_id=(mate, my), device_id_type=MESH)
    gate_begin(0, gacc[...])
    key_alone(cap, mid_b)
    rows_out = by_head(att_hbm, cs, 4, True) + by_head(dq_hbm, qs, 4 + heads, True)
    for copy in rows_out:
        copy.start()

    pl.semaphore_wait(free, 1)
    settled = list(started)
    started.clear()
    dv_out = []

    def dv_done():
        dv_last()
        dv_out.append(finish(0, dv_hbm, 2))

    partials(
        1,
        k_mate,
        (
            [dv_done],
            [lambda: gate_begin(1, gate_end(0))] + dk_events[:2],
            dk_events[2:4],
            [lambda: gate_begin(2, gate_end(1))],
            [],
        ),
    )
    for make in settled:
        make().wait_send()
    for event in dk_events[4:6]:
        event()
    gate_begin(3, gate_end(2))
    for event in dk_events[6:8]:
        event()
    dk_events[8]()
    dk_events[9]()
    grand = jnp.sum(gate_end(3))
    slope = (1.0 - gate_tanh * gate_tanh) * grand / math.sqrt(total_elems)
    gate_out[0] = slope[0, 0]
    for event in dk_events[10:]:
        event()

    def drain(p, carry):
        v_mate(p).wait_send()
        k_mate(p).wait_send()
        return carry

    lax.fori_loop(0, spans // 2, drain, 0)
    dk_last()
    dk_out = finish(1, dk_hbm, 3)
    flush()
    for copy in rows_out + [dk_out] + dv_out:
        copy.wait()


def body(queries, image_keys, image_values, span_tiles, gate_logit, cotangent):
    tok_count, columns = queries.shape
    spans = span_tiles.shape[0]
    span_len = tok_count // spans
    heads = columns // HEAD
    image_len = image_keys.shape[1]
    tile_count = lax.axis_size("seq")
    total_elems = tok_count * tile_count * columns * lax.axis_size("mp")
    smem = pl.BlockSpec(memory_space=pltpu.SMEM)
    hbm = pl.BlockSpec(memory_space=pl.ANY)
    sizes = (spans, span_len, heads, image_len, total_elems)
    rows = heads * span_len
    kv = (tile_count, image_len, HEAD)
    by_span = (spans, span_len, columns)
    att, dq, dk, dv, gate = pl.pallas_call(
        functools.partial(kernel, sizes),
        out_shape=(
            jax.ShapeDtypeStruct(by_span, BF16),
            jax.ShapeDtypeStruct(by_span, BF16),
            jax.ShapeDtypeStruct(image_keys.shape, BF16),
            jax.ShapeDtypeStruct(image_values.shape, BF16),
            jax.ShapeDtypeStruct((1,), F32),
        ),
        in_specs=[smem, smem, hbm, hbm, hbm, hbm],
        out_specs=(hbm, hbm, hbm, hbm, smem),
        scratch_shapes=[
            pltpu.VMEM(kv, BF16),
            pltpu.VMEM(kv, BF16),
            pltpu.VMEM((spans, rows, image_len), BF16),
            pltpu.VMEM((spans, rows, HEAD), BF16),
            pltpu.VMEM((spans + 1, rows, HEAD), BF16),
            pltpu.VMEM((spans, rows, HEAD), BF16),
            pltpu.VMEM((spans + 1, HEAD, image_len), BF16),
            pltpu.VMEM((2, tile_count, HEAD, image_len), BF16),
            pltpu.VMEM((2, HEAD), jnp.int32),
            pltpu.SMEM((2, HEAD), jnp.int32),
            pltpu.VMEM((tile_count // 2, 2, HEAD // 2, image_len), BF16),
            pltpu.VMEM((2, RING, 2, 2, HEAD // 4, image_len), BF16),
            pltpu.VMEM((2, RING, 2, 2, HEAD // 2, image_len), BF16),
            pltpu.VMEM((2, 2, 2, HEAD // 4, image_len), BF16),
            pltpu.VMEM((2, 2, 2, HEAD // 2, image_len), BF16),
            pltpu.VMEM((2, HEAD // 2, image_len), BF16),
            pltpu.VMEM((2, image_len, HEAD), BF16),
            pltpu.VMEM((rows, image_len), F32),
            pltpu.VMEM((rows, image_len), F32),
            pltpu.VMEM((rows, HEAD), BF16),
            pltpu.VMEM((rows, HEAD), BF16),
            pltpu.VMEM((rows, image_len), BF16),
            pltpu.VMEM((rows, image_len), BF16),
            pltpu.VMEM((8, HEAD), F32),
            pltpu.VMEM((4, RING, 8, HEAD), F32),
            pltpu.SemaphoreType.DMA((180,)),
            pltpu.SemaphoreType.DMA((180,)),
            pltpu.SemaphoreType.DMA((4 + 2 * heads,)),
            pltpu.SemaphoreType.REGULAR,
        ],
        compiler_params=pltpu.CompilerParams(
            collective_id=0, has_side_effects=True, vmem_limit_bytes=67043328
        ),
        name="cross_attention",
    )(
        span_tiles.reshape(spans),
        gate_logit,
        queries.reshape(by_span),
        image_keys,
        image_values,
        cotangent.reshape(by_span),
    )
    gate_tanh = jnp.tanh(gate_logit[0])
    attended = (gate_tanh * att.reshape(queries.shape).astype(F32)).astype(BF16)
    return (attended, dq.reshape(queries.shape), dk, dv, gate)


def solution(mesh):
    placed = (
        P("seq", "mp"),
        P("seq", None, "mp"),
        P("seq", None, "mp"),
        P("seq", None),
        P(),
        P("seq", "mp"),
    )
    return jax.shard_map(
        body,
        mesh=mesh,
        in_specs=placed,
        out_specs=(P("seq", "mp"), P("seq", "mp"), P("seq", None, "mp"), P("seq", None, "mp"), P()),
        check_vma=False,
    )
```

```python
import functools
import math

import jax
import jax.numpy as jnp
from jax import lax
from jax.experimental import pallas as pl
from jax.experimental.pallas import tpu as pltpu
from jax.sharding import PartitionSpec as P

HEAD = 128
RING = 4
LOG2E = 1.4426950408889634
MESH = pl.DeviceIdType.MESH
F32 = jnp.float32
BF16 = jnp.bfloat16


def nt(left, right):
    return lax.dot_general(left, right, (((1,), (1,)), ((), ())), preferred_element_type=F32)


def nn(left, right):
    return lax.dot_general(left, right, (((1,), (0,)), ((), ())), preferred_element_type=F32)


def tn(left, right):
    return lax.dot_general(left, right, (((0,), (0,)), ((), ())), preferred_element_type=F32)


def wrap(value):
    return lax.rem(value + RING, RING)


def kernel(
    sizes,
    tiles,
    gate,
    q_hbm,
    k_hbm,
    v_hbm,
    c_hbm,
    att_hbm,
    dq_hbm,
    dk_hbm,
    dv_hbm,
    gate_out,
    kall,
    vall,
    probs,
    cs,
    qs,
    gs,
    alone,
    part,
    slots_v,
    slots,
    l3,
    lb1,
    lb2,
    la1,
    la2,
    l0,
    upright,
    wide_a,
    wide_b,
    thin_a,
    thin_b,
    mid_a,
    mid_b,
    gacc,
    gland,
    send,
    recv,
    loc,
    free,
):
    spans, span_len, heads, image_len, total_elems = sizes
    scale = 1.0 / math.sqrt(HEAD)
    me = lax.axis_index("seq")
    my = lax.axis_index("mp")
    z = lax.div(me, 8)
    x = lax.rem(lax.div(me, 2), RING)
    c = lax.rem(me, 2)
    mate = me + 1 - 2 * c
    a = z * (1 - c) + x * c
    b = x * (1 - c) + z * c
    stride_a = 4 - 3 * c
    stride_b = 1 + 3 * c

    def pair(da, db):
        return wrap(a + da) * stride_a + wrap(b + db) * stride_b

    def mate_pair(da, db):
        return wrap(b + da) * stride_b + wrap(a + db) * stride_a

    def at(da, db):
        return (2 * pair(da, db) + c, my)

    barrier = pltpu.get_barrier_semaphore()
    friends = [(mate, my)]
    for d in range(1, RING):
        friends.append((8 * wrap(z + d) + 2 * x + c, my))
        friends.append((8 * z + 2 * wrap(x + d) + c, my))
        friends.append((me, wrap(my + d)))
    for friend in friends:
        pl.semaphore_signal(barrier, inc=1, device_id=friend, device_id_type=MESH)

    def by_head(hbm, buf, index, out):
        copies = []
        for h in range(heads):
            flat_side = hbm.at[:, :, pl.ds(h * HEAD, HEAD)]
            head_side = buf.at[pl.ds(0, spans), pl.ds(h * span_len, span_len), :]
            src, dst = (head_side, flat_side) if out else (flat_side, head_side)
            copies.append(pltpu.make_async_copy(src, dst, loc.at[index + h]))
        return copies

    k_in = pltpu.make_async_copy(k_hbm, kall.at[pl.ds(me, 1)], loc.at[0])
    v_in = pltpu.make_async_copy(v_hbm, vall.at[pl.ds(me, 1)], loc.at[1])
    rows_in = by_head(q_hbm, qs, 4, False) + by_head(c_hbm, cs, 4 + heads, False)
    k_in.start()
    v_in.start()
    for copy in rows_in:
        copy.start()
    pl.semaphore_wait(barrier, len(friends))

    started = []

    def remote(src, dst, index, target):
        return pltpu.make_async_remote_copy(
            src_ref=src,
            dst_ref=dst,
            send_sem=send.at[index],
            recv_sem=recv.at[index],
            device_id=target,
            device_id_type=MESH,
        )

    def start(make):
        make().start()
        started.append(make)

    half = image_len // 2
    quarter = half // 2
    steps = (0, -1, 1, 2)

    def gather(buf, base):
        mine, other = c * half, (1 - c) * half

        def piece(which, first, rows):
            return buf.at[pl.ds(2 * which, 2), pl.ds(pl.multiple_of(first, 64), rows), :]

        def own_copy(first, tile, index):
            ref = buf.at[pl.ds(tile, 1), pl.ds(pl.multiple_of(first, 64), half), :]
            return remote(ref, ref, base + index, (mate, my))

        def moved(which, direction, index, target, narrow):
            if narrow:
                ref = piece(which, mine + direction * quarter, quarter)
            else:
                ref = piece(which, mine, half)
            return remote(ref, ref, base + index, target)

        def to_mate(k, kb):
            ref = piece(pair(steps[k], steps[kb]), mine, half)
            return remote(ref, ref, base + 24 + 4 * k + kb, (mate, my))

        def from_mate(k, kb):
            ref = piece(mate_pair(steps[k], steps[kb]), other, half)
            return remote(ref, ref, base + 24 + 4 * k + kb, (mate, my))

        sign = (1, -1)

        def lone(tile, index, target):
            ref = buf.at[pl.ds(tile, 1), pl.ds(pl.multiple_of(mine, 64), half), :]
            return remote(ref, ref, base + index, target)

        def lone_a(tile, d, second):
            return lone(tile, (40 if second else 2) + d, at(sign[d], 0))

        def lone_b(tile, d, second):
            return lone(tile, (42 if second else 8) + d, at(0, sign[d]))

        def e0():
            start(lambda: own_copy(other, me, 0))
            for d in range(2):
                start(lambda d=d: lone_a(me, d, False))
                start(lambda d=d: lone_b(me, d, False))
            start(lambda: own_copy(mine, me, 1))

        def send_b(k):
            for d in range(2):
                start(lambda d=d: moved(pair(steps[k], 0), d, 8 + 4 * k + d, at(0, sign[d]), False))

        def e1():
            own_copy(mine, mate, 0).wait_recv()
            for d in range(2):
                start(lambda d=d: lone_a(mate, d, True))
                start(lambda d=d: lone_b(mate, d, True))

        def e_a(d):
            lone_a(2 * pair(-sign[d], 0) + c, d, False).wait_recv()
            lone_a(2 * pair(-sign[d], 0) + 1 - c, d, True).wait_recv()
            start(lambda: moved(pair(-sign[d], 0), d, 4 + d, at(sign[d], 0), True))
            send_b(1 + d)
            start(lambda: to_mate(1 + d, 0))

        def e_aq():
            for d in range(2):
                moved(pair(2, 0), d, 4 + d, at(sign[d], 0), True).wait_recv()
            send_b(3)
            start(lambda: to_mate(3, 0))

        def e_b(k, d):
            if k == 0:
                lone_b(2 * pair(0, -sign[d]) + c, d, False).wait_recv()
                lone_b(2 * pair(0, -sign[d]) + 1 - c, d, True).wait_recv()
            else:
                moved(pair(steps[k], -sign[d]), d, 8 + 4 * k + d, at(0, sign[d]), False).wait_recv()
            start(
                lambda: moved(
                    pair(steps[k], -sign[d]), d, 10 + 4 * k + d, at(0, sign[d]), True
                )
            )
            start(lambda: to_mate(k, 1 + d))

        def e_bq(k):
            for d in range(2):
                moved(pair(steps[k], 2), d, 10 + 4 * k + d, at(0, sign[d]), True).wait_recv()
            start(lambda: to_mate(k, 3))

        def e_end():
            own_copy(other, mate, 1).wait_recv()
            for k in range(4):
                for kb in range(4):
                    if k or kb:
                        from_mate(k, kb).wait_recv()

        events = [
            lambda: e_a(0),
            lambda: e_a(1),
            lambda: e_b(0, 0),
            lambda: e_b(0, 1),
            e_aq,
            lambda: e_b(1, 0),
            lambda: e_b(1, 1),
            lambda: e_b(2, 0),
            lambda: e_b(2, 1),
            lambda: e_bq(0),
            lambda: e_b(3, 0),
            lambda: e_b(3, 1),
            lambda: e_bq(1),
            lambda: e_bq(2),
            lambda: e_bq(3),
        ]
        return e0, e1, events, e_end

    lane_half = HEAD // 2
    lane_quarter = HEAD // 4

    def reduce(y, base):
        mine, other = c * lane_half, (1 - c) * lane_half

        def piece(which, first, rows):
            return part.at[y, pl.ds(2 * which, 2), pl.ds(pl.multiple_of(first, 32), rows), :]

        def landing(which):
            if y == 0:
                return l3.at[which]
            return probs.at[pl.ds(2 * which, 2), pl.ds(0, lane_half), :]

        def to_mate(which):
            return remote(piece(which, other, lane_half), landing(which), base + which, (mate, my))

        def add(which, first, rows, *landed):
            view = (y, pl.ds(2 * which, 2), pl.ds(pl.multiple_of(first, 32), rows), slice(None))
            total = part[view].astype(F32)
            for ref in landed:
                total = total + ref[...].astype(F32)
            part[view] = total.astype(BF16)

        def fold(which):
            to_mate(which).wait_recv()
            add(which, mine, lane_half, landing(which))

        def near(which, d, land, index, target, narrow):
            if narrow:
                ref = piece(which, mine + d * lane_quarter, lane_quarter)
            else:
                ref = piece(which, mine, lane_half)
            return remote(ref, land, base + index, target)

        sign = (-1, 1)

        def first_b(k, d):
            return near(pair(k, 2), d, lb1.at[y, k, d], 16 + 4 * k + d, at(0, sign[d]), True)

        def second_b(k, d):
            return near(pair(k, sign[d]), d, lb2.at[y, k, d], 18 + 4 * k + d, at(0, sign[d]), False)

        def first_a(d):
            return near(pair(2, 0), d, la1.at[y, d], 32 + d, at(sign[d], 0), True)

        def second_a(d):
            return near(pair(sign[d], 0), d, la2.at[y, d], 34 + d, at(sign[d], 0), False)

        def r1(k):
            fold(pair(k, 2))
            for d in range(2):
                start(lambda d=d: first_b(k, d))

        def r2(k):
            for d in range(2):
                fold(pair(k, sign[d]))
                first_b(k, d).wait_recv()
                add(pair(k, sign[d]), mine + d * lane_quarter, lane_quarter, lb1.at[y, k, d])
                start(lambda d=d: second_b(k, d))

        def r3(k):
            fold(pair(k, 0))
            for d in range(2):
                second_b(k, d).wait_recv()
            add(pair(k, 0), mine, lane_half, lb2.at[y, k, 0], lb2.at[y, k, 1])
            if k == 2:
                for d in range(2):
                    start(lambda d=d: first_a(d))
            if k in (1, 3):
                d = 0 if k == 3 else 1
                first_a(d).wait_recv()
                add(pair(sign[d], 0), mine + d * lane_quarter, lane_quarter, la1.at[y, d])
                start(lambda: second_a(d))

        def last():
            def make(first, tile):
                ref = part.at[y, tile, pl.ds(pl.multiple_of(first, 32), lane_half), :]
                return remote(ref, l0.at[y], base + 36, (mate, my))

            for d in range(2):
                second_a(d).wait_recv()
            add(pair(0, 0), mine, lane_half, la2.at[y, 0], la2.at[y, 1])
            start(lambda: make(mine, mate))
            make(mine, mate).wait_recv()

        order = (2, 3, 1, 0)
        events = [functools.partial(r1, k) for k in order]
        events += [functools.partial(r2, k) for k in order]
        events += [functools.partial(r3, k) for k in order]
        return to_mate, events, last

    def finish(y, hbm, index):
        mine, other = c * lane_half, (1 - c) * lane_half
        mid_a[pl.ds(pl.multiple_of(mine, 32), lane_half), :] = part[
            y, me, pl.ds(pl.multiple_of(mine, 32), lane_half), :
        ]
        mid_a[pl.ds(pl.multiple_of(other, 32), lane_half), :] = l0[y]
        upright[y] = mid_a[0:HEAD, :].T
        copy = pltpu.make_async_copy(upright.at[pl.ds(y, 1)], hbm, loc.at[index])
        copy.start()
        return copy

    k0, k1, k_events, k_end = gather(kall, 0)
    v0, v1, v_events, v_end = gather(vall, 44)
    v_mate, dv_events, dv_last = reduce(0, 88)
    k_mate, dk_events, dk_last = reduce(1, 128)

    def run(step, total, cuts):
        low = 0
        for high, events in cuts:
            if high > low:
                lax.fori_loop(low, high, step, 0)
            low = high
            for event in events:
                event()
        if low < total:
            lax.fori_loop(low, total, step, 0)

    def flush():
        for make in started:
            make().wait_send()
        started.clear()

    rings = (
        (c, [(mate, my)]),
        (z, [(8 * wrap(z + d) + 2 * x + c, my) for d in range(1, RING)]),
        (x, [(8 * z + 2 * wrap(x + d) + c, my) for d in range(1, RING)]),
        (my, [(me, wrap(my + d)) for d in range(1, RING)]),
    )
    gate_base = 168

    def gate_copy(stage, d):
        own, targets = rings[stage]
        ref = gland.at[stage, own]
        return remote(ref, ref, gate_base + 3 * stage + d, targets[d])

    def gate_begin(stage, value):
        own, targets = rings[stage]
        gland[stage, own] = value
        for d in range(len(targets)):
            start(lambda d=d: gate_copy(stage, d))

    def gate_end(stage):
        own, targets = rings[stage]
        for d in range(len(targets)):
            gate_copy(stage, d).wait_recv()
        total = gland[stage, 0]
        for i in range(1, len(targets) + 1):
            total = total + gland[stage, i]
        return total

    k_in.wait()
    k0()
    lane = lax.broadcasted_iota(jnp.int32, (1, HEAD), 1)
    first = final = jnp.full((1, HEAD), spans, jnp.int32)
    for s in range(spans):
        hit = lane == tiles[s]
        final = jnp.where(hit, s, final)
        first = jnp.where(hit & (first == spans), s, first)
    slots_v[0:1, :] = first
    slots_v[1:2, :] = jnp.where(final > first, final, spans)
    slots_copy = pltpu.make_async_copy(slots_v, slots, loc.at[2])
    slots_copy.start()
    gate_tanh = jnp.tanh(jnp.full((8, HEAD), gate[0], F32))
    tanh_row = jnp.broadcast_to(gate_tanh[0:1, 0:1], (heads * span_len, HEAD))
    gacc[...] = jnp.zeros((8, HEAD), F32)
    alone[spans] = jnp.zeros((HEAD, image_len), BF16)
    qs[spans] = jnp.zeros((heads * span_len, HEAD), BF16)
    mid_b[...] = jnp.zeros((heads * span_len, image_len), BF16)
    k1()
    v_in.wait()
    v0()
    for event in k_events[:9]:
        event()
    for copy in rows_in:
        copy.wait()

    def gated(s, carry):
        gs[s] = (tanh_row * cs[s].astype(F32)).astype(BF16)
        return carry

    lax.fori_loop(0, spans, gated, 0)
    for event in k_events[9:12]:
        event()
    v1()
    for event in k_events[12:]:
        event()
    k_end()

    cap = spans - 1

    def score(s, wide):
        wide[...] = nt(qs[s], kall[tiles[s]])

    def soften(s, wide, mid):
        scores = wide[...]
        top = jnp.max(scores, axis=1, keepdims=True)
        expo = jnp.exp2((scores - top) * (scale * LOG2E))
        inv = 1.0 / jnp.sum(expo, axis=1, keepdims=True)
        weights = (expo * inv).astype(BF16)
        probs[s] = weights
        mid[...] = weights

    def before(i):
        return jnp.where(i == 0, spans, 2 * i - 1)

    def value_alone(s, mid):
        alone[s] = tn(gs[jnp.minimum(s, cap)], mid[...]).astype(BF16)

    def soften_two(i, carry):
        score(2 * i + 1, wide_b)
        value_alone(before(i), mid_b)
        soften(2 * i, wide_a, mid_a)
        score(jnp.minimum(2 * i + 2, cap), wide_a)
        value_alone(2 * i, mid_a)
        soften(2 * i + 1, wide_b, mid_b)
        return carry

    score(0, wide_a)
    run(
        soften_two,
        spans // 2,
        (
            (4, v_events[:4]),
            (9, v_events[4:5]),
            (13, v_events[5:9]),
            (16, v_events[9:10]),
        ),
    )

    value_alone(cap, mid_b)
    mid_b[...] = jnp.zeros((heads * span_len, image_len), BF16)

    slots_copy.wait()

    def partials(y, mate_copy, cuts):
        def add_pair(which):
            for i in range(2):
                tile = 2 * which + i
                both = alone[slots[0, tile]].astype(F32) + alone[slots[1, tile]].astype(F32)
                part[y, tile] = both.astype(BF16)
            mate_copy(which).start()

        def along_x(i, carry):
            add_pair(RING * wrap(z + 2) + wrap(x + i))
            return carry

        def along_z(i, carry):
            add_pair(RING * wrap(z + 3 + i) + wrap(x + 2))
            return carry

        def inner(u):
            def step(i, carry):
                add_pair(RING * wrap(z + u) + wrap(x + 3 + i))
                return carry

            return step

        loops = [(along_x, 4), (along_z, 3), (inner(3), 3), (inner(1), 3), (inner(0), 3)]
        for (step, count), events in zip(loops, cuts):
            lax.fori_loop(0, count, step, 0)
            for event in events:
                event()

    partials(
        0,
        v_mate,
        (v_events[10:12], dv_events[:2], dv_events[2:4] + v_events[12:13], v_events[13:14], ()),
    )
    v_events[14]()
    v_end()

    def spread(s, wide, thin):
        values = vall[tiles[s]]
        wide[...] = nt(gs[s], values)
        thin[...] = nn(probs[s], values).astype(BF16)

    def backward(s, wide, thin, mid):
        attn_f = thin[...].astype(F32)
        delta = jnp.sum(gs[s].astype(F32) * attn_f, axis=1, keepdims=True)
        mid[...] = (probs[s].astype(F32) * (wide[...] - delta) * scale).astype(BF16)
        product = cs[s].astype(F32) * attn_f
        cs[s] = (tanh_row * attn_f).astype(BF16)
        gacc[...] += sum(product[8 * i : 8 * i + 8] for i in range(heads * span_len // 8))

    def key_alone(s, mid):
        dscore = mid[...]
        alone[s] = tn(qs[s], dscore).astype(BF16)
        qs[s] = nn(dscore, kall[tiles[jnp.minimum(s, cap)]]).astype(BF16)

    def backward_two(i, carry):
        spread(2 * i + 1, wide_b, thin_b)
        key_alone(before(i), mid_b)
        backward(2 * i, wide_a, thin_a, mid_a)
        spread(jnp.minimum(2 * i + 2, cap), wide_a, thin_a)
        key_alone(2 * i, mid_a)
        backward(2 * i + 1, wide_b, thin_b, mid_b)
        return carry

    spread(0, wide_a, thin_a)
    run(
        backward_two,
        spans // 2,
        (
            (2, dv_events[4:6]),
            (4, dv_events[6:8]),
            (7, dv_events[8:9]),
            (11, dv_events[9:11]),
            (14, dv_events[11:12]),
            (16, ()),
        ),
    )
    pl.semaphore_signal(free, inc=1, device_id=(mate, my), device_id_type=MESH)
    gate_begin(0, gacc[...])
    key_alone(cap, mid_b)
    rows_out = by_head(att_hbm, cs, 4, True) + by_head(dq_hbm, qs, 4 + heads, True)
    for copy in rows_out:
        copy.start()

    pl.semaphore_wait(free, 1)
    settled = list(started)
    started.clear()
    dv_out = []

    def dv_done():
        dv_last()
        dv_out.append(finish(0, dv_hbm, 2))

    partials(
        1,
        k_mate,
        (
            [dv_done],
            [lambda: gate_begin(1, gate_end(0))] + dk_events[:2],
            dk_events[2:4],
            [lambda: gate_begin(2, gate_end(1))],
            [],
        ),
    )
    for make in settled:
        make().wait_send()
    for event in dk_events[4:6]:
        event()
    gate_begin(3, gate_end(2))
    for event in dk_events[6:8]:
        event()
    dk_events[8]()
    dk_events[9]()
    grand = jnp.sum(gate_end(3))
    slope = (1.0 - gate_tanh * gate_tanh) * grand / math.sqrt(total_elems)
    gate_out[0] = slope[0, 0]
    for event in dk_events[10:]:
        event()

    def drain(p, carry):
        v_mate(p).wait_send()
        k_mate(p).wait_send()
        return carry

    lax.fori_loop(0, spans // 2, drain, 0)
    dk_last()
    dk_out = finish(1, dk_hbm, 3)
    flush()
    for copy in rows_out + [dk_out] + dv_out:
        copy.wait()


def body(queries, image_keys, image_values, span_tiles, gate_logit, cotangent):
    tok_count, columns = queries.shape
    spans = span_tiles.shape[0]
    span_len = tok_count // spans
    heads = columns // HEAD
    image_len = image_keys.shape[1]
    tile_count = lax.axis_size("seq")
    total_elems = tok_count * tile_count * columns * lax.axis_size("mp")
    smem = pl.BlockSpec(memory_space=pltpu.SMEM)
    hbm = pl.BlockSpec(memory_space=pl.ANY)
    sizes = (spans, span_len, heads, image_len, total_elems)
    rows = heads * span_len
    kv = (tile_count, image_len, HEAD)
    by_span = (spans, span_len, columns)
    att, dq, dk, dv, gate = pl.pallas_call(
        functools.partial(kernel, sizes),
        out_shape=(
            jax.ShapeDtypeStruct(by_span, BF16),
            jax.ShapeDtypeStruct(by_span, BF16),
            jax.ShapeDtypeStruct(image_keys.shape, BF16),
            jax.ShapeDtypeStruct(image_values.shape, BF16),
            jax.ShapeDtypeStruct((1,), F32),
        ),
        in_specs=[smem, smem, hbm, hbm, hbm, hbm],
        out_specs=(hbm, hbm, hbm, hbm, smem),
        scratch_shapes=[
            pltpu.VMEM(kv, BF16),
            pltpu.VMEM(kv, BF16),
            pltpu.VMEM((spans, rows, image_len), BF16),
            pltpu.VMEM((spans, rows, HEAD), BF16),
            pltpu.VMEM((spans + 1, rows, HEAD), BF16),
            pltpu.VMEM((spans, rows, HEAD), BF16),
            pltpu.VMEM((spans + 1, HEAD, image_len), BF16),
            pltpu.VMEM((2, tile_count, HEAD, image_len), BF16),
            pltpu.VMEM((2, HEAD), jnp.int32),
            pltpu.SMEM((2, HEAD), jnp.int32),
            pltpu.VMEM((tile_count // 2, 2, HEAD // 2, image_len), BF16),
            pltpu.VMEM((2, RING, 2, 2, HEAD // 4, image_len), BF16),
            pltpu.VMEM((2, RING, 2, 2, HEAD // 2, image_len), BF16),
            pltpu.VMEM((2, 2, 2, HEAD // 4, image_len), BF16),
            pltpu.VMEM((2, 2, 2, HEAD // 2, image_len), BF16),
            pltpu.VMEM((2, HEAD // 2, image_len), BF16),
            pltpu.VMEM((2, image_len, HEAD), BF16),
            pltpu.VMEM((rows, image_len), F32),
            pltpu.VMEM((rows, image_len), F32),
            pltpu.VMEM((rows, HEAD), BF16),
            pltpu.VMEM((rows, HEAD), BF16),
            pltpu.VMEM((rows, image_len), BF16),
            pltpu.VMEM((rows, image_len), BF16),
            pltpu.VMEM((8, HEAD), F32),
            pltpu.VMEM((4, RING, 8, HEAD), F32),
            pltpu.SemaphoreType.DMA((180,)),
            pltpu.SemaphoreType.DMA((180,)),
            pltpu.SemaphoreType.DMA((4 + 2 * heads,)),
            pltpu.SemaphoreType.REGULAR,
        ],
        compiler_params=pltpu.CompilerParams(
            collective_id=0, has_side_effects=True, vmem_limit_bytes=67043328
        ),
        name="cross_attention",
    )(
        span_tiles.reshape(spans),
        gate_logit,
        queries.reshape(by_span),
        image_keys,
        image_values,
        cotangent.reshape(by_span),
    )
    return (att.reshape(queries.shape), dq.reshape(queries.shape), dk, dv, gate)


def solution(mesh):
    placed = (
        P("seq", "mp"),
        P("seq", None, "mp"),
        P("seq", None, "mp"),
        P("seq", None),
        P(),
        P("seq", "mp"),
    )
    return jax.shard_map(
        body,
        mesh=mesh,
        in_specs=placed,
        out_specs=(P("seq", "mp"), P("seq", "mp"), P("seq", None, "mp"), P("seq", None, "mp"), P()),
        check_vma=False,
    )
```

```python
import functools
import math

import jax
import jax.numpy as jnp
from jax import lax
from jax.experimental import pallas as pl
from jax.experimental.pallas import tpu as pltpu
from jax.sharding import PartitionSpec as P

HEAD = 128
RING = 4
LOG2E = 1.4426950408889634
MESH = pl.DeviceIdType.MESH
F32 = jnp.float32
BF16 = jnp.bfloat16


def nt(left, right):
    return lax.dot_general(left, right, (((1,), (1,)), ((), ())), preferred_element_type=F32)


def nn(left, right):
    return lax.dot_general(left, right, (((1,), (0,)), ((), ())), preferred_element_type=F32)


def tn(left, right):
    return lax.dot_general(left, right, (((0,), (0,)), ((), ())), preferred_element_type=F32)


def wrap(value):
    return lax.rem(value + RING, RING)


def kernel(
    sizes,
    tiles,
    gate,
    q_hbm,
    k_hbm,
    v_hbm,
    c_hbm,
    att_hbm,
    dq_hbm,
    dk_hbm,
    dv_hbm,
    gate_out,
    kall,
    vall,
    probs,
    cs,
    qs,
    gs,
    alone,
    part,
    slots_v,
    slots,
    l3,
    lb1,
    lb2,
    la1,
    la2,
    l0,
    upright,
    wide_a,
    wide_b,
    thin_a,
    thin_b,
    mid_a,
    mid_b,
    gacc,
    gland,
    send,
    recv,
    loc,
    free,
):
    spans, span_len, heads, image_len, total_elems = sizes
    scale = 1.0 / math.sqrt(HEAD)
    me = lax.axis_index("seq")
    my = lax.axis_index("mp")
    z = lax.div(me, 8)
    x = lax.rem(lax.div(me, 2), RING)
    c = lax.rem(me, 2)
    mate = me + 1 - 2 * c
    a = z * (1 - c) + x * c
    b = x * (1 - c) + z * c
    stride_a = 4 - 3 * c
    stride_b = 1 + 3 * c

    def pair(da, db):
        return wrap(a + da) * stride_a + wrap(b + db) * stride_b

    def mate_pair(da, db):
        return wrap(b + da) * stride_b + wrap(a + db) * stride_a

    def at(da, db):
        return (2 * pair(da, db) + c, my)

    barrier = pltpu.get_barrier_semaphore()
    friends = [(mate, my)]
    for d in range(1, RING):
        friends.append((8 * wrap(z + d) + 2 * x + c, my))
        friends.append((8 * z + 2 * wrap(x + d) + c, my))
        friends.append((me, wrap(my + d)))
    for friend in friends:
        pl.semaphore_signal(barrier, inc=1, device_id=friend, device_id_type=MESH)

    def by_head(hbm, buf, index, out):
        copies = []
        for h in range(heads):
            flat_side = hbm.at[:, :, pl.ds(h * HEAD, HEAD)]
            head_side = buf.at[pl.ds(0, spans), pl.ds(h * span_len, span_len), :]
            src, dst = (head_side, flat_side) if out else (flat_side, head_side)
            copies.append(pltpu.make_async_copy(src, dst, loc.at[index + h]))
        return copies

    k_in = pltpu.make_async_copy(k_hbm, kall.at[pl.ds(me, 1)], loc.at[0])
    v_in = pltpu.make_async_copy(v_hbm, vall.at[pl.ds(me, 1)], loc.at[1])
    rows_in = by_head(q_hbm, qs, 4, False) + by_head(c_hbm, cs, 4 + heads, False)
    k_in.start()
    v_in.start()
    for copy in rows_in:
        copy.start()
    pl.semaphore_wait(barrier, len(friends))

    started = []

    def remote(src, dst, index, target):
        return pltpu.make_async_remote_copy(
            src_ref=src,
            dst_ref=dst,
            send_sem=send.at[index],
            recv_sem=recv.at[index],
            device_id=target,
            device_id_type=MESH,
        )

    def start(make):
        make().start()
        started.append(make)

    half = image_len // 2
    quarter = half // 2
    steps = (0, -1, 1, 2)

    def gather(buf, base):
        mine, other = c * half, (1 - c) * half

        def piece(which, first, rows):
            return buf.at[pl.ds(2 * which, 2), pl.ds(pl.multiple_of(first, 64), rows), :]

        def own_copy(first, tile, index):
            ref = buf.at[pl.ds(tile, 1), pl.ds(pl.multiple_of(first, 64), half), :]
            return remote(ref, ref, base + index, (mate, my))

        def moved(which, direction, index, target, narrow):
            if narrow:
                ref = piece(which, mine + direction * quarter, quarter)
            else:
                ref = piece(which, mine, half)
            return remote(ref, ref, base + index, target)

        def to_mate(k, kb):
            ref = piece(pair(steps[k], steps[kb]), mine, half)
            return remote(ref, ref, base + 24 + 4 * k + kb, (mate, my))

        def from_mate(k, kb):
            ref = piece(mate_pair(steps[k], steps[kb]), other, half)
            return remote(ref, ref, base + 24 + 4 * k + kb, (mate, my))

        sign = (1, -1)

        def lone(tile, index, target):
            ref = buf.at[pl.ds(tile, 1), pl.ds(pl.multiple_of(mine, 64), half), :]
            return remote(ref, ref, base + index, target)

        def lone_a(tile, d, second):
            return lone(tile, (40 if second else 2) + d, at(sign[d], 0))

        def lone_b(tile, d, second):
            return lone(tile, (42 if second else 8) + d, at(0, sign[d]))

        def e0():
            start(lambda: own_copy(other, me, 0))
            for d in range(2):
                start(lambda d=d: lone_a(me, d, False))
                start(lambda d=d: lone_b(me, d, False))
            start(lambda: own_copy(mine, me, 1))

        def send_b(k):
            for d in range(2):
                start(lambda d=d: moved(pair(steps[k], 0), d, 8 + 4 * k + d, at(0, sign[d]), False))

        def e1():
            own_copy(mine, mate, 0).wait_recv()
            for d in range(2):
                start(lambda d=d: lone_a(mate, d, True))
                start(lambda d=d: lone_b(mate, d, True))

        def e_a(d):
            lone_a(2 * pair(-sign[d], 0) + c, d, False).wait_recv()
            lone_a(2 * pair(-sign[d], 0) + 1 - c, d, True).wait_recv()
            start(lambda: moved(pair(-sign[d], 0), d, 4 + d, at(sign[d], 0), True))
            send_b(1 + d)
            start(lambda: to_mate(1 + d, 0))

        def e_aq():
            for d in range(2):
                moved(pair(2, 0), d, 4 + d, at(sign[d], 0), True).wait_recv()
            send_b(3)
            start(lambda: to_mate(3, 0))

        def e_b(k, d):
            if k == 0:
                lone_b(2 * pair(0, -sign[d]) + c, d, False).wait_recv()
                lone_b(2 * pair(0, -sign[d]) + 1 - c, d, True).wait_recv()
            else:
                moved(pair(steps[k], -sign[d]), d, 8 + 4 * k + d, at(0, sign[d]), False).wait_recv()
            start(
                lambda: moved(
                    pair(steps[k], -sign[d]), d, 10 + 4 * k + d, at(0, sign[d]), True
                )
            )
            start(lambda: to_mate(k, 1 + d))

        def e_bq(k):
            for d in range(2):
                moved(pair(steps[k], 2), d, 10 + 4 * k + d, at(0, sign[d]), True).wait_recv()
            start(lambda: to_mate(k, 3))

        def e_end():
            own_copy(other, mate, 1).wait_recv()
            for k in range(4):
                for kb in range(4):
                    if k or kb:
                        from_mate(k, kb).wait_recv()

        events = [
            lambda: e_a(0),
            lambda: e_a(1),
            lambda: e_b(0, 0),
            lambda: e_b(0, 1),
            e_aq,
            lambda: e_b(1, 0),
            lambda: e_b(1, 1),
            lambda: e_b(2, 0),
            lambda: e_b(2, 1),
            lambda: e_bq(0),
            lambda: e_b(3, 0),
            lambda: e_b(3, 1),
            lambda: e_bq(1),
            lambda: e_bq(2),
            lambda: e_bq(3),
        ]
        return e0, e1, events, e_end

    lane_half = HEAD // 2
    lane_quarter = HEAD // 4

    def reduce(y, base):
        mine, other = c * lane_half, (1 - c) * lane_half

        def piece(which, first, rows):
            return part.at[y, pl.ds(2 * which, 2), pl.ds(pl.multiple_of(first, 32), rows), :]

        def landing(which):
            if y == 0:
                return l3.at[which]
            return probs.at[pl.ds(2 * which, 2), pl.ds(0, lane_half), :]

        def to_mate(which):
            return remote(piece(which, other, lane_half), landing(which), base + which, (mate, my))

        def add(which, first, rows, *landed):
            view = (y, pl.ds(2 * which, 2), pl.ds(pl.multiple_of(first, 32), rows), slice(None))
            total = part[view].astype(F32)
            for ref in landed:
                total = total + ref[...].astype(F32)
            part[view] = total.astype(BF16)

        def fold(which):
            to_mate(which).wait_recv()
            add(which, mine, lane_half, landing(which))

        def near(which, d, land, index, target, narrow):
            if narrow:
                ref = piece(which, mine + d * lane_quarter, lane_quarter)
            else:
                ref = piece(which, mine, lane_half)
            return remote(ref, land, base + index, target)

        sign = (-1, 1)

        def first_b(k, d):
            return near(pair(k, 2), d, lb1.at[y, k, d], 16 + 4 * k + d, at(0, sign[d]), True)

        def second_b(k, d):
            return near(pair(k, sign[d]), d, lb2.at[y, k, d], 18 + 4 * k + d, at(0, sign[d]), False)

        def first_a(d):
            return near(pair(2, 0), d, la1.at[y, d], 32 + d, at(sign[d], 0), True)

        def second_a(d):
            return near(pair(sign[d], 0), d, la2.at[y, d], 34 + d, at(sign[d], 0), False)

        def r1(k):
            fold(pair(k, 2))
            for d in range(2):
                start(lambda d=d: first_b(k, d))

        def r2(k):
            for d in range(2):
                fold(pair(k, sign[d]))
                first_b(k, d).wait_recv()
                add(pair(k, sign[d]), mine + d * lane_quarter, lane_quarter, lb1.at[y, k, d])
                start(lambda d=d: second_b(k, d))

        def r3(k):
            fold(pair(k, 0))
            for d in range(2):
                second_b(k, d).wait_recv()
            add(pair(k, 0), mine, lane_half, lb2.at[y, k, 0], lb2.at[y, k, 1])
            if k == 2:
                for d in range(2):
                    start(lambda d=d: first_a(d))
            if k in (1, 3):
                d = 0 if k == 3 else 1
                first_a(d).wait_recv()
                add(pair(sign[d], 0), mine + d * lane_quarter, lane_quarter, la1.at[y, d])
                start(lambda: second_a(d))

        def last():
            def make(first, tile):
                ref = part.at[y, tile, pl.ds(pl.multiple_of(first, 32), lane_half), :]
                return remote(ref, l0.at[y], base + 36, (mate, my))

            for d in range(2):
                second_a(d).wait_recv()
            add(pair(0, 0), mine, lane_half, la2.at[y, 0], la2.at[y, 1])
            start(lambda: make(mine, mate))
            make(mine, mate).wait_recv()

        order = (2, 3, 1, 0)
        events = [functools.partial(r1, k) for k in order]
        events += [functools.partial(r2, k) for k in order]
        events += [functools.partial(r3, k) for k in order]
        return to_mate, events, last

    def finish(y, hbm, index):
        mine, other = c * lane_half, (1 - c) * lane_half
        mid_a[pl.ds(pl.multiple_of(mine, 32), lane_half), :] = part[
            y, me, pl.ds(pl.multiple_of(mine, 32), lane_half), :
        ]
        mid_a[pl.ds(pl.multiple_of(other, 32), lane_half), :] = l0[y]
        upright[y] = mid_a[0:HEAD, :].T
        copy = pltpu.make_async_copy(upright.at[pl.ds(y, 1)], hbm, loc.at[index])
        copy.start()
        return copy

    k0, k1, k_events, k_end = gather(kall, 0)
    v0, v1, v_events, v_end = gather(vall, 44)
    v_mate, dv_events, dv_last = reduce(0, 88)
    k_mate, dk_events, dk_last = reduce(1, 128)

    def run(step, total, cuts):
        low = 0
        for high, events in cuts:
            if high > low:
                lax.fori_loop(low, high, step, 0)
            low = high
            for event in events:
                event()
        if low < total:
            lax.fori_loop(low, total, step, 0)

    def flush():
        for make in started:
            make().wait_send()
        started.clear()

    rings = (
        (c, [(mate, my)]),
        (z, [(8 * wrap(z + d) + 2 * x + c, my) for d in range(1, RING)]),
        (x, [(8 * z + 2 * wrap(x + d) + c, my) for d in range(1, RING)]),
        (my, [(me, wrap(my + d)) for d in range(1, RING)]),
    )
    gate_base = 168

    def gate_copy(stage, d):
        own, targets = rings[stage]
        ref = gland.at[stage, own]
        return remote(ref, ref, gate_base + 3 * stage + d, targets[d])

    def gate_begin(stage, value):
        own, targets = rings[stage]
        gland[stage, own] = value
        for d in range(len(targets)):
            start(lambda d=d: gate_copy(stage, d))

    def gate_end(stage):
        own, targets = rings[stage]
        for d in range(len(targets)):
            gate_copy(stage, d).wait_recv()
        total = gland[stage, 0]
        for i in range(1, len(targets) + 1):
            total = total + gland[stage, i]
        return total

    k_in.wait()
    k0()
    lane = lax.broadcasted_iota(jnp.int32, (1, HEAD), 1)
    first = final = jnp.full((1, HEAD), spans, jnp.int32)
    for s in range(spans):
        hit = lane == tiles[s]
        final = jnp.where(hit, s, final)
        first = jnp.where(hit & (first == spans), s, first)
    slots_v[0:1, :] = first
    slots_v[1:2, :] = jnp.where(final > first, final, spans)
    slots_copy = pltpu.make_async_copy(slots_v, slots, loc.at[2])
    slots_copy.start()
    gate_tanh = jnp.tanh(jnp.full((8, HEAD), gate[0], F32))
    tanh_row = jnp.broadcast_to(gate_tanh[0:1, 0:1], (heads * span_len, HEAD))
    gacc[...] = jnp.zeros((8, HEAD), F32)
    alone[spans] = jnp.zeros((HEAD, image_len), BF16)
    qs[spans] = jnp.zeros((heads * span_len, HEAD), BF16)
    mid_b[...] = jnp.zeros((heads * span_len, image_len), BF16)
    k1()
    v_in.wait()
    v0()
    for event in k_events[:9]:
        event()
    for copy in rows_in:
        copy.wait()

    def gated(s, carry):
        gs[s] = (tanh_row * cs[s].astype(F32)).astype(BF16)
        return carry

    lax.fori_loop(0, spans, gated, 0)
    for event in k_events[9:12]:
        event()
    v1()
    for event in k_events[12:]:
        event()
    k_end()

    cap = spans - 1

    def score(s, wide):
        wide[...] = nt(qs[s], kall[tiles[s]])

    def soften(s, wide, mid):
        scores = wide[...]
        top = jnp.max(scores, axis=1, keepdims=True)
        expo = jnp.exp2((scores - top) * (scale * LOG2E))
        inv = 1.0 / jnp.sum(expo, axis=1, keepdims=True)
        weights = (expo * inv).astype(BF16)
        probs[s] = weights
        mid[...] = weights

    def before(i):
        return jnp.where(i == 0, spans, 2 * i - 1)

    def value_alone(s, mid):
        alone[s] = tn(gs[jnp.minimum(s, cap)], mid[...]).astype(BF16)

    def soften_two(i, carry):
        score(2 * i + 1, wide_b)
        value_alone(before(i), mid_b)
        soften(2 * i, wide_a, mid_a)
        score(jnp.minimum(2 * i + 2, cap), wide_a)
        value_alone(2 * i, mid_a)
        soften(2 * i + 1, wide_b, mid_b)
        return carry

    score(0, wide_a)
    run(
        soften_two,
        spans // 2,
        (
            (4, v_events[:4]),
            (9, v_events[4:5]),
            (13, v_events[5:9]),
            (16, v_events[9:10]),
        ),
    )

    value_alone(cap, mid_b)
    mid_b[...] = jnp.zeros((heads * span_len, image_len), BF16)

    slots_copy.wait()

    def partials(y, mate_copy, cuts):
        def add_pair(which):
            for i in range(2):
                tile = 2 * which + i
                both = alone[slots[0, tile]].astype(F32) + alone[slots[1, tile]].astype(F32)
                part[y, tile] = both.astype(BF16)
            mate_copy(which).start()

        def along_x(i, carry):
            add_pair(RING * wrap(z + 2) + wrap(x + i))
            return carry

        def along_z(i, carry):
            add_pair(RING * wrap(z + 3 + i) + wrap(x + 2))
            return carry

        def inner(u):
            def step(i, carry):
                add_pair(RING * wrap(z + u) + wrap(x + 3 + i))
                return carry

            return step

        loops = [(along_x, 4), (along_z, 3), (inner(3), 3), (inner(1), 3), (inner(0), 3)]
        for (step, count), events in zip(loops, cuts):
            lax.fori_loop(0, count, step, 0)
            for event in events:
                event()

    partials(
        0,
        v_mate,
        (v_events[10:12], dv_events[:2], dv_events[2:4] + v_events[12:13], v_events[13:14], ()),
    )
    v_events[14]()
    v_end()

    def spread(s, wide, thin):
        values = vall[tiles[s]]
        wide[...] = nt(gs[s], values)
        thin[...] = nn(probs[s], values).astype(BF16)

    def backward(s, wide, thin, mid):
        attn_f = thin[...].astype(F32)
        delta = jnp.sum(gs[s].astype(F32) * attn_f, axis=1, keepdims=True)
        mid[...] = (probs[s].astype(F32) * (wide[...] - delta) * scale).astype(BF16)
        product = cs[s].astype(F32) * attn_f
        cs[s] = (tanh_row * attn_f).astype(BF16)
        gacc[...] += sum(product[8 * i : 8 * i + 8] for i in range(heads * span_len // 8))

    def key_alone(s, mid):
        dscore = mid[...]
        alone[s] = tn(qs[s], dscore).astype(BF16)
        qs[s] = nn(dscore, kall[tiles[jnp.minimum(s, cap)]]).astype(BF16)

    def backward_two(i, carry):
        spread(2 * i + 1, wide_b, thin_b)
        key_alone(before(i), mid_b)
        backward(2 * i, wide_a, thin_a, mid_a)
        spread(jnp.minimum(2 * i + 2, cap), wide_a, thin_a)
        key_alone(2 * i, mid_a)
        backward(2 * i + 1, wide_b, thin_b, mid_b)
        return carry

    spread(0, wide_a, thin_a)
    run(
        backward_two,
        spans // 2,
        (
            (2, dv_events[4:6]),
            (4, dv_events[6:8]),
            (7, dv_events[8:9]),
            (11, dv_events[9:11]),
            (14, dv_events[11:12]),
            (16, ()),
        ),
    )
    pl.semaphore_signal(free, inc=1, device_id=(mate, my), device_id_type=MESH)
    gate_begin(0, gacc[...])
    key_alone(cap, mid_b)
    rows_out = by_head(att_hbm, cs, 4, True) + by_head(dq_hbm, qs, 4 + heads, True)
    for copy in rows_out:
        copy.start()

    pl.semaphore_wait(free, 1)
    settled = list(started)
    started.clear()
    dv_out = []

    def dv_done():
        dv_last()
        dv_out.append(finish(0, dv_hbm, 2))

    partials(
        1,
        k_mate,
        (
            [dv_done],
            [lambda: gate_begin(1, gate_end(0))] + dk_events[:2],
            dk_events[2:4],
            [lambda: gate_begin(2, gate_end(1))],
            [],
        ),
    )
    for make in settled:
        make().wait_send()
    for event in dk_events[4:6]:
        event()
    gate_begin(3, gate_end(2))
    for event in dk_events[6:8]:
        event()
    dk_events[8]()
    dk_events[9]()
    for event in dk_events[10:]:
        event()
    grand = jnp.sum(gate_end(3))
    slope = (1.0 - gate_tanh * gate_tanh) * grand / math.sqrt(total_elems)
    gate_out[0] = slope[0, 0]

    def drain(p, carry):
        v_mate(p).wait_send()
        k_mate(p).wait_send()
        return carry

    lax.fori_loop(0, spans // 2, drain, 0)
    dk_last()
    dk_out = finish(1, dk_hbm, 3)
    flush()
    for copy in rows_out + [dk_out] + dv_out:
        copy.wait()


def body(queries, image_keys, image_values, span_tiles, gate_logit, cotangent):
    tok_count, columns = queries.shape
    spans = span_tiles.shape[0]
    span_len = tok_count // spans
    heads = columns // HEAD
    image_len = image_keys.shape[1]
    tile_count = lax.axis_size("seq")
    total_elems = tok_count * tile_count * columns * lax.axis_size("mp")
    smem = pl.BlockSpec(memory_space=pltpu.SMEM)
    hbm = pl.BlockSpec(memory_space=pl.ANY)
    sizes = (spans, span_len, heads, image_len, total_elems)
    rows = heads * span_len
    kv = (tile_count, image_len, HEAD)
    by_span = (spans, span_len, columns)
    att, dq, dk, dv, gate = pl.pallas_call(
        functools.partial(kernel, sizes),
        out_shape=(
            jax.ShapeDtypeStruct(by_span, BF16),
            jax.ShapeDtypeStruct(by_span, BF16),
            jax.ShapeDtypeStruct(image_keys.shape, BF16),
            jax.ShapeDtypeStruct(image_values.shape, BF16),
            jax.ShapeDtypeStruct((1,), F32),
        ),
        in_specs=[smem, smem, hbm, hbm, hbm, hbm],
        out_specs=(hbm, hbm, hbm, hbm, smem),
        scratch_shapes=[
            pltpu.VMEM(kv, BF16),
            pltpu.VMEM(kv, BF16),
            pltpu.VMEM((spans, rows, image_len), BF16),
            pltpu.VMEM((spans, rows, HEAD), BF16),
            pltpu.VMEM((spans + 1, rows, HEAD), BF16),
            pltpu.VMEM((spans, rows, HEAD), BF16),
            pltpu.VMEM((spans + 1, HEAD, image_len), BF16),
            pltpu.VMEM((2, tile_count, HEAD, image_len), BF16),
            pltpu.VMEM((2, HEAD), jnp.int32),
            pltpu.SMEM((2, HEAD), jnp.int32),
            pltpu.VMEM((tile_count // 2, 2, HEAD // 2, image_len), BF16),
            pltpu.VMEM((2, RING, 2, 2, HEAD // 4, image_len), BF16),
            pltpu.VMEM((2, RING, 2, 2, HEAD // 2, image_len), BF16),
            pltpu.VMEM((2, 2, 2, HEAD // 4, image_len), BF16),
            pltpu.VMEM((2, 2, 2, HEAD // 2, image_len), BF16),
            pltpu.VMEM((2, HEAD // 2, image_len), BF16),
            pltpu.VMEM((2, image_len, HEAD), BF16),
            pltpu.VMEM((rows, image_len), F32),
            pltpu.VMEM((rows, image_len), F32),
            pltpu.VMEM((rows, HEAD), BF16),
            pltpu.VMEM((rows, HEAD), BF16),
            pltpu.VMEM((rows, image_len), BF16),
            pltpu.VMEM((rows, image_len), BF16),
            pltpu.VMEM((8, HEAD), F32),
            pltpu.VMEM((4, RING, 8, HEAD), F32),
            pltpu.SemaphoreType.DMA((180,)),
            pltpu.SemaphoreType.DMA((180,)),
            pltpu.SemaphoreType.DMA((4 + 2 * heads,)),
            pltpu.SemaphoreType.REGULAR,
        ],
        compiler_params=pltpu.CompilerParams(
            collective_id=0, has_side_effects=True, vmem_limit_bytes=67043328
        ),
        name="cross_attention",
    )(
        span_tiles.reshape(spans),
        gate_logit,
        queries.reshape(by_span),
        image_keys,
        image_values,
        cotangent.reshape(by_span),
    )
    return (att.reshape(queries.shape), dq.reshape(queries.shape), dk, dv, gate)


def solution(mesh):
    placed = (
        P("seq", "mp"),
        P("seq", None, "mp"),
        P("seq", None, "mp"),
        P("seq", None),
        P(),
        P("seq", "mp"),
    )
    return jax.shard_map(
        body,
        mesh=mesh,
        in_specs=placed,
        out_specs=(P("seq", "mp"), P("seq", "mp"), P("seq", None, "mp"), P("seq", None, "mp"), P()),
        check_vma=False,
    )
```
